32 devices in a mesh: gx: 4 (over z), gy: 4 (over y, x), gz: 2 (over core).
Axes of the slice: x: 2, y: 2, z: 4, core: 2. Of those that a mesh axis runs over, the one named last changes fastest.
Arguments:
- velocity: float32 [3, 64, 64, 256], P(None, 'gx', 'gy', 'gz'), may hold values from -6 to 6
Outputs:
- stress_residual: float32 [6, 2048], P(None, ('gx', 'gy', 'gz'))
- coefficients: float32 [96, 6], replicated
The draws below stay inside these ranges and needn't reach their ends.
All inputs are finite; a program needn't handle non-finite values.
Results may differ from the reference program's by a relative error of at most 0.0042.
Values may be sent and summed in bfloat16 or wider, within the bound.
No kernel may reach another device: no remote copies, remote signals or barrier semaphores. Data moves between devices by JAX's collectives and lax.ppermute only.
A program may use at most 64 MiB of HBM per device.

```python
import jax
import jax.numpy as jnp
import numpy as np
from jax import lax

BX = 16
BY = 16
BZ = 128
NX = 64
NY = 64
NZ = 256
SAMPLES = 2048
N_GX = 4
N_GY = 4
N_GZ = 2


def levels(key, dims, pieces, least, high):
    gain, own = 1.0, jax.random.fold_in(key, 6)
    for position, blocks in pieces:
        steps = jnp.exp(jax.random.uniform(jax.random.fold_in(own, position), (blocks,), jnp.float32, least / len(pieces), high / len(pieces)))
        gain = gain * jnp.repeat(steps, dims[position] // blocks).reshape([-1 if axis == position else 1 for axis in range(len(dims))])
    return gain


def normal_values(own_key, extent, scale, limit, split=(), kind=jnp.bfloat16):
    array = scale * jax.random.normal(own_key, extent, jnp.float32)
    if split:
        array = array * levels(own_key, extent, split, -0.22, 0.18)
    return jnp.clip(array, -limit, limit).astype(kind)


def setup_inputs(seed: int = 0) -> dict:
    keys = jax.random.split(jax.random.key(seed), 2)
    velocity = normal_values(keys[0], (3, NX, NY, NZ), 1.0, 6.0, ((1, 4), (2, 4), (3, 2)), jnp.float32)
    return {"velocity": velocity}


PRECISE = lax.Precision.HIGHEST
INDEX_PAIRS = ((0, 0), (1, 1), (2, 2), (0, 1), (0, 2), (1, 2))
WIDTHS = (3.0, 6.0, 12.0)

def window_table(combos):
    weights_table = np.zeros((len(combos), 16), np.float32)
    for row_index in range(len(combos)):
        box_width, offset = combos[row_index]
        low_edge = 7.5 + offset - box_width / 2.0
        high_edge = 7.5 + offset + box_width / 2.0
        for cell_index in range(16):
            cell_share = min(cell_index + 0.5, high_edge) - max(cell_index - 0.5, low_edge)
            weights_table[row_index, cell_index] = max(cell_share, 0.0) / box_width
    return weights_table

def velocity_combos():
    return [(box_width, offset) for box_width in WIDTHS for offset in (-2.0, 0.0, 2.0)]

def product_combos():
    return [(3.0, 0.0), (12.0, 0.0)]

def matrix_product(left_matrix, right_matrix):
    return [[left_matrix[i][0] * right_matrix[0][j] + left_matrix[i][1] * right_matrix[1][j] + left_matrix[i][2] * right_matrix[2][j] for j in range(3)] for i in range(3)]

def pick_pairs(matrix):
    return [matrix[i][j] for i, j in INDEX_PAIRS]

def build_rows(box_means, pair_means):
    feature_rows = []
    centre_values = []
    for width_index in range(3):
        middle = 3 * width_index + 1
        scaled = WIDTHS[width_index] ** 2 * 0.25

        def offset_value(component, direction, step_size):
            position_list = [middle, middle, middle]
            position_list[direction] = middle + step_size
            return box_means[component, position_list[0], position_list[1], position_list[2]]
        centre_values.append([box_means[i, middle, middle, middle] for i in range(3)])
        gradient = [[(offset_value(i, j, 1) - offset_value(i, j, -1)) * scaled for j in range(3)] for i in range(3)]
        strain = [[(gradient[i][j] + gradient[j][i]) * 0.5 for j in range(3)] for i in range(3)]
        spin_part = [[(gradient[i][j] - gradient[j][i]) * 0.5 for j in range(3)] for i in range(3)]
        square_strain = matrix_product(strain, strain)
        first_order = matrix_product(strain, spin_part)
        second_order = matrix_product(spin_part, strain)
        commutator = [[first_order[i][j] - second_order[i][j] for j in range(3)] for i in range(3)]
        spin_square = matrix_product(spin_part, spin_part)
        magnitude = sum((strain[i][j] * strain[i][j] for i in range(3) for j in range(3)))
        feature_rows += pick_pairs(strain) + pick_pairs(square_strain) + pick_pairs(commutator) + pick_pairs(spin_square)
        feature_rows += [magnitude * entry for entry in pick_pairs(strain)]
    small_box = centre_values[0]
    large_box = centre_values[2]
    feature_rows += [pair_means[index, 0] - small_box[i] * small_box[j] for index, (i, j) in enumerate(INDEX_PAIRS)]
    target_rows = [pair_means[index, 1] - large_box[i] * large_box[j] for index, (i, j) in enumerate(INDEX_PAIRS)]
    return (jnp.stack(feature_rows), jnp.stack(target_rows))

def solve_fit(gram_matrix, sample_total):
    scales = jnp.sqrt(jnp.diagonal(gram_matrix) / sample_total + 1e-06)
    feature_scale = scales[:96]
    normal = gram_matrix[:96, :96] / (sample_total * feature_scale[:, None] * feature_scale[None, :]) + 0.1 * jnp.eye(96, dtype=jnp.float32)
    target_side = gram_matrix[:96, 96:] / (sample_total * feature_scale[:, None])
    factor = jnp.linalg.cholesky(normal)
    solved = jax.scipy.linalg.cho_solve((factor, True), target_side)
    return (solved / feature_scale[:, None], scales[96:])

def reference(velocity):
    rounded = lax.optimization_barrier(velocity.astype(jnp.bfloat16)).astype(jnp.float32)
    count_x, count_y, count_z = (NX // 8, NY // 8, NZ // 8)
    offsets = jnp.arange(16, dtype=jnp.int32) - 4
    y_index = (8 * jnp.arange(count_y, dtype=jnp.int32)[:, None] + offsets[None, :]) % NY
    z_index = (8 * jnp.arange(count_z, dtype=jnp.int32)[:, None] + offsets[None, :]) % NZ
    speed_table = jnp.asarray(window_table(velocity_combos()), dtype=jnp.float32)
    pair_table = jnp.asarray(window_table(product_combos()), dtype=jnp.float32)

    def windowed(slab_cells, weights_table):
        along_z = jnp.einsum('cxyzw,kw->cxyzk', slab_cells[:, :, :, z_index], weights_table, precision=PRECISE)
        along_y = jnp.einsum('cxbvzk,jv->cxbjzk', along_z[:, :, y_index], weights_table, precision=PRECISE)
        return jnp.einsum('cxbjzk,ix->cibjzk', along_y, weights_table, precision=PRECISE)

    def one_slab(slab_index):
        x_index = (8 * slab_index + offsets) % NX
        slab_cells = jnp.take(rounded, x_index, axis=1)
        box_means = windowed(slab_cells, speed_table)
        box_means = jnp.transpose(box_means, (0, 1, 3, 5, 2, 4)).reshape(3, 9, 9, 9, count_y * count_z)
        pair_slab = jnp.stack([slab_cells[i] * slab_cells[j] for i, j in INDEX_PAIRS])
        pair_means = windowed(pair_slab, pair_table)
        pair_means = jnp.stack([pair_means[:, 0, :, 0, :, 0], pair_means[:, 1, :, 1, :, 1]], axis=1)
        pair_means = pair_means.reshape(6, 2, count_y * count_z)
        features, targets = build_rows(box_means, pair_means)
        return jnp.concatenate([features, targets], axis=0)
    stacked = lax.map(one_slab, jnp.arange(count_x, dtype=jnp.int32))
    gram_matrix = jnp.einsum('aif,ajf->ij', stacked, stacked, precision=PRECISE)
    coefficients, target_scale = solve_fit(gram_matrix, float(SAMPLES))
    predicted = jnp.einsum('ik,aif->akf', coefficients, stacked[:, :96], precision=PRECISE)
    residual = (stacked[:, 96:] - predicted) / target_scale[None, :, None]
    residual = residual.reshape(N_GX, BX // 8, 6, N_GY, BY // 8, N_GZ, BZ // 8)
    residual = jnp.transpose(residual, (2, 0, 3, 5, 1, 4, 6)).reshape(6, SAMPLES)
    return (residual, coefficients)
```

```python
import functools

import jax
import jax.numpy as jnp
import numpy as np
from jax import lax
from jax.experimental import pallas as pl
from jax.experimental.pallas import tpu as pltpu
from jax.sharding import PartitionSpec as P

PRECISE = lax.Precision.HIGHEST
INDEX_PAIRS = ((0, 0), (1, 1), (2, 2), (0, 1), (0, 2), (1, 2))
WIDTHS = (3.0, 6.0, 12.0)


def extended(block, sides, width):
    for axis, dim in sides:
        count = lax.axis_size(axis)
        forward = [(i, i + 1) for i in range(count - 1)]
        forward.append((count - 1, 0))
        backward = [(target, source) for source, target in forward]
        low = lax.ppermute(
            lax.slice_in_dim(block, block.shape[dim] - width, None, axis=dim), axis, forward
        )
        high = lax.ppermute(lax.slice_in_dim(block, 0, width, axis=dim), axis, backward)
        block = jnp.concatenate([low, block, high], axis=dim)
    return block


def window_table(combos):
    weights_table = np.zeros((len(combos), 16), np.float32)
    for row_index in range(len(combos)):
        box_width, offset = combos[row_index]
        low_edge = 7.5 + offset - box_width / 2.0
        high_edge = 7.5 + offset + box_width / 2.0
        for cell_index in range(16):
            cell_share = min(cell_index + 0.5, high_edge) - max(cell_index - 0.5, low_edge)
            weights_table[row_index, cell_index] = max(cell_share, 0.0) / box_width
    return weights_table


def velocity_combos():
    return [(box_width, offset) for box_width in WIDTHS for offset in (-2.0, 0.0, 2.0)]


def product_combos():
    return [(3.0, 0.0), (12.0, 0.0)]


def matrix_product(left_matrix, right_matrix):
    return [
        [
            left_matrix[i][0] * right_matrix[0][j]
            + left_matrix[i][1] * right_matrix[1][j]
            + left_matrix[i][2] * right_matrix[2][j]
            for j in range(3)
        ]
        for i in range(3)
    ]


def pick_pairs(matrix):
    return [matrix[i][j] for i, j in INDEX_PAIRS]


def build_rows(box_means, pair_means):
    feature_rows = []
    centre_values = []
    for width_index in range(3):
        middle = 3 * width_index + 1
        scaled = WIDTHS[width_index] ** 2 * 0.25

        def offset_value(component, direction, step_size):
            position_list = [middle, middle, middle]
            position_list[direction] = middle + step_size
            return box_means[component, position_list[0], position_list[1], position_list[2]]

        centre_values.append([box_means[i, middle, middle, middle] for i in range(3)])
        gradient = [
            [(offset_value(i, j, 1) - offset_value(i, j, -1)) * scaled for j in range(3)]
            for i in range(3)
        ]
        strain = [[(gradient[i][j] + gradient[j][i]) * 0.5 for j in range(3)] for i in range(3)]
        spin_part = [[(gradient[i][j] - gradient[j][i]) * 0.5 for j in range(3)] for i in range(3)]
        square_strain = matrix_product(strain, strain)
        first_order = matrix_product(strain, spin_part)
        second_order = matrix_product(spin_part, strain)
        commutator = [[first_order[i][j] - second_order[i][j] for j in range(3)] for i in range(3)]
        spin_square = matrix_product(spin_part, spin_part)
        magnitude = sum((strain[i][j] * strain[i][j] for i in range(3) for j in range(3)))
        feature_rows += (
            pick_pairs(strain)
            + pick_pairs(square_strain)
            + pick_pairs(commutator)
            + pick_pairs(spin_square)
        )
        feature_rows += [magnitude * entry for entry in pick_pairs(strain)]
    small_box = centre_values[0]
    large_box = centre_values[2]
    feature_rows += [
        pair_means[index, 0] - small_box[i] * small_box[j]
        for index, (i, j) in enumerate(INDEX_PAIRS)
    ]
    target_rows = [
        pair_means[index, 1] - large_box[i] * large_box[j]
        for index, (i, j) in enumerate(INDEX_PAIRS)
    ]
    return (jnp.stack(feature_rows), jnp.stack(target_rows))


def solve_fit(gram_matrix, sample_total):
    scales = jnp.sqrt(jnp.diagonal(gram_matrix) / sample_total + 1e-06)
    feature_scale = scales[:96]
    normal = gram_matrix[:96, :96] / (
        sample_total * feature_scale[:, None] * feature_scale[None, :]
    ) + 0.1 * jnp.eye(96, dtype=jnp.float32)
    target_side = gram_matrix[:96, 96:] / (sample_total * feature_scale[:, None])
    factor = jnp.linalg.cholesky(normal)
    solved = jax.scipy.linalg.cho_solve((factor, True), target_side)
    return (solved / feature_scale[:, None], scales[96:])


def axis_weights(length, weights_table):
    sample_count = length // 8
    combo_count = weights_table.shape[0]
    full_table = np.zeros((sample_count * combo_count, length + 8), np.float32)
    for sample_index in range(sample_count):
        full_table[
            sample_index * combo_count : (sample_index + 1) * combo_count,
            8 * sample_index : 8 * sample_index + 16,
        ] = weights_table
    return jnp.asarray(full_table)


def windowed(wide_field, weights_table):
    along_z = jnp.einsum(
        "cxyz,kz->cxyk",
        wide_field,
        axis_weights(wide_field.shape[3] - 8, weights_table),
        precision=PRECISE,
    )
    along_y = jnp.einsum(
        "cxyk,jy->cxjk",
        along_z,
        axis_weights(wide_field.shape[2] - 8, weights_table),
        precision=PRECISE,
    )
    return jnp.einsum(
        "cxjk,ix->cijk",
        along_y,
        axis_weights(wide_field.shape[1] - 8, weights_table),
        precision=PRECISE,
    )


def shards(velocity):
    rounded = velocity.astype(jnp.bfloat16)
    padded = extended(rounded, (("gx", 1), ("gy", 2), ("gz", 3)), 4)
    wide_field = padded.astype(jnp.float32)
    count_x = velocity.shape[1] // 8
    count_y = velocity.shape[2] // 8
    count_z = velocity.shape[3] // 8
    samples = count_x * count_y * count_z
    box_means = windowed(wide_field, window_table(velocity_combos()))
    box_means = box_means.reshape(3, count_x, 9, count_y, 9, count_z, 9)
    box_means = jnp.transpose(box_means, (0, 2, 4, 6, 1, 3, 5)).reshape(3, 9, 9, 9, samples)
    pair_field = jnp.stack([wide_field[i] * wide_field[j] for i, j in INDEX_PAIRS])
    pair_means = windowed(pair_field, window_table(product_combos())).reshape(
        6, count_x, 2, count_y, 2, count_z, 2
    )
    pair_means = jnp.stack(
        [pair_means[:, :, 0, :, 0, :, 0], pair_means[:, :, 1, :, 1, :, 1]], axis=1
    )
    pair_means = pair_means.reshape(6, 2, samples)
    features, targets = build_rows(box_means, pair_means)
    stacked = jnp.concatenate([features, targets], axis=0)
    local_gram = jnp.dot(stacked, stacked.T, precision=PRECISE, preferred_element_type=jnp.float32)
    gram_matrix = lax.psum(local_gram, ("gx", "gy", "gz"))
    sample_total = float(samples * lax.axis_size("gx") * lax.axis_size("gy") * lax.axis_size("gz"))
    coefficients, target_scale = solve_fit(gram_matrix, sample_total)
    predicted = jnp.dot(
        coefficients.T, features, precision=PRECISE, preferred_element_type=jnp.float32
    )
    residual = (targets - predicted) / target_scale[:, None]
    return (residual, coefficients)


WAYS = (0.0, 2.0, -2.0, 0.0, 0.0, 0.0, 0.0)
YWAYS = (0.0, 0.0, 0.0, 2.0, -2.0, 0.0, 0.0)
OWN = ((0, 0), (0, 1), (1, 0), (1, 1))
FACE_LOW = ((-1, -1), (-1, 2), (-1, 0), (-1, 1))
FACE_HIGH = ((2, 0), (2, 1), (2, -1), (2, 2))
FACE_Y = ((1, -1), (1, 2), (0, -1), (0, 2))


def share(centre, width, cell):
    part = min(cell + 0.5, centre + width / 2) - max(cell - 0.5, centre - width / 2)
    return max(part, 0.0)


def plane_row(bx, by, width, place, shift):
    along_x = [share(8 * place[0] + 3.5 + shift[0], width, n) for n in range(bx)]
    along_y = [share(8 * place[1] + 3.5 + shift[1], width, n) for n in range(by)]
    return np.outer(along_x, along_y).reshape(-1)


def velocity_plane_table(bx, by):
    rows = []

    def add(place, entries):
        for entry in entries:
            if entry is None:
                rows.append(np.zeros(bx * by))
            else:
                rows.append(plane_row(bx, by, entry[0], place, (entry[1], entry[2])))

    centre = (12.0, 0.0, 0.0)
    for width in WIDTHS:
        for place in OWN:
            add(place, [(width, WAYS[q], YWAYS[q]) for q in range(7)] + [None])
    for places in (FACE_LOW, FACE_HIGH):
        for place in places:
            low = places is FACE_LOW
            first = (12.0 if low else 6.0, 2.0 if low else -2.0, 0.0)
            second = (6.0 if low else 12.0, 2.0 if low else -2.0, 0.0)
            if place[1] in (0, 1):
                third, fourth = (12.0, 0.0, 2.0), (12.0, 0.0, -2.0)
            else:
                third, fourth = (12.0, 0.0, 2.0 if place[1] < 0 else -2.0), None
            add(place, [centre, first, second, third, fourth, centre, centre, None])
    for place in FACE_Y:
        step = 2.0 if place[1] < 0 else -2.0
        add(
            place,
            [centre, (12.0, 2.0, 0.0), (12.0, -2.0, 0.0), (12.0, 0.0, step), (6.0, 0.0, step)]
            + [centre, centre, None],
        )
    return np.stack(rows)


def pair_plane_table(bx, by):
    rows = []
    for width, places in ((3.0, OWN), (12.0, OWN + FACE_LOW + FACE_HIGH + FACE_Y)):
        for place in places:
            rows.append(plane_row(bx, by, width, place, (0.0, 0.0)))
    while len(rows) % 16:
        rows.append(np.zeros(bx * by))
    return np.stack(rows)


def line_table(length, width, extra):
    samples = length // 8
    table = np.zeros((length, 4 * samples))
    blocks = [(width, 0.0), (width, 2.0), (width, -2.0)] + ([(extra, 0.0)] if extra else [])
    for block, (box, shift) in enumerate(blocks):
        for sample in range(samples):
            for cell in range(length):
                for turn in (-1, 0, 1):
                    table[cell, block * samples + sample] += share(
                        8 * sample + 3.5 + shift, box, cell + turn * length
                    )
    return table


def three_parts(value):
    high = value.astype(jnp.bfloat16)
    rest = value - high.astype(jnp.float32)
    middle = rest.astype(jnp.bfloat16)
    low = (rest - middle.astype(jnp.float32)).astype(jnp.bfloat16)
    return high, middle, low


def mxu(left, right):
    return jnp.dot(left, right, preferred_element_type=jnp.float32)


def sums_kernel(x_ref, wv_ref, wp_ref, l3_ref, l6_ref, l12_ref, out_ref, pair_ref):
    core = lax.axis_index("gz")
    cells = x_ref.shape[1] * x_ref.shape[2]
    length = x_ref.shape[3]
    begin = pl.multiple_of(core * length, length)
    lines = [ref[pl.ds(begin, length), :] for ref in (l3_ref, l6_ref, l12_ref)]
    doubled = [jnp.concatenate([line, line], axis=0) for line in lines]

    def along_line(value, which):
        high, middle, low = three_parts(value)
        return mxu(jnp.concatenate([high, middle], axis=1), doubled[which]) + mxu(low, lines[which])

    rows = lax.broadcasted_iota(jnp.int32, (8, 128), 0)
    lanes = lax.broadcasted_iota(jnp.int32, (8, 128), 1) // 32

    def gathered(groups, row_block):
        total = jnp.zeros((8, 128), jnp.float32)
        for place in range(4):
            merged = groups[8 * place : 8 * place + 8]
            base = merged
            for row, block in row_block.items():
                merged = jnp.where(rows == row, pltpu.roll(base, (128 - 32 * block) % 128, 1), merged)
            if place:
                merged = pltpu.roll(merged, 32 * place, 1)
            total = jnp.where(lanes == place, merged, total)
        return total

    fields = [x_ref[c].reshape(cells, length).astype(jnp.bfloat16) for c in range(3)]
    ends = {5: 1, 6: 2}
    faces = ({5: 1, 6: 2, 2: 3}, {5: 1, 6: 2, 1: 3}, {5: 1, 6: 2, 4: 3})
    for c in range(3):
        plane = mxu(wv_ref[...], fields[c])
        for which in range(3):
            line = along_line(plane[32 * which : 32 * which + 32], which)
            out_ref[pl.ds((which * 3 + c) * 8, 8), :] = gathered(line, ends)
        line = along_line(plane[96:192], 2)
        for face in range(3):
            out_ref[pl.ds(88 + 32 * face + 8 * c, 8), :] = gathered(
                line[32 * face : 32 * face + 32], faces[face]
            )
    wide = [field.astype(jnp.float32) for field in fields]
    pair_ref[...] = jnp.zeros(pair_ref.shape, jnp.float32)
    count = wp_ref.shape[0]
    weights = jnp.concatenate([wp_ref[...], wp_ref[...]], axis=1)
    for pair, (i, j) in enumerate(INDEX_PAIRS):
        product = wide[i] * wide[j]
        high = product.astype(jnp.bfloat16)
        low = (product - high.astype(jnp.float32)).astype(jnp.bfloat16)
        pair_ref[pl.ds(pair, count, stride=8), :] = mxu(
            weights, jnp.concatenate([high, low], axis=0)
        )
    out_ref[pl.ds(72, 8), :] = gathered(along_line(pair_ref[pl.ds(0, 32), :], 0), {})
    line = along_line(pair_ref[pl.ds(32, 128), :], 2)
    out_ref[pl.ds(80, 8), :] = gathered(line[0:32], {})
    for face in range(3):
        out_ref[pl.ds(112 + 32 * face, 8), :] = gathered(line[32 * face + 32 : 32 * face + 64], {})


def features_kernel(f_ref, low_ref, high_ref, next_ref, prev_ref, z_ref, gram_ref, s_ref):
    rows = lax.broadcasted_iota(jnp.int32, (8, 128), 0)
    lane = lax.broadcasted_iota(jnp.int32, (8, 128), 1)
    right = lane >= 64
    upper = (lane // 32) % 2 == 1
    keep = jnp.logical_not(((rows == 1) & (lane < 64)) | ((rows == 2) & right))
    zero = jnp.zeros((8, 128), jnp.float32)

    def along_x(at):
        return jnp.where(right, low_ref[pl.ds(at, 8), :], high_ref[pl.ds(at, 8), :])

    def along_y(at):
        after = pltpu.roll(next_ref[pl.ds(at, 8), :], 96, 1)
        before = pltpu.roll(prev_ref[pl.ds(at, 8), :], 32, 1)
        return jnp.where(upper, after, before)

    for c in range(3):
        s_ref[pl.ds(8 * c, 8), :] = f_ref[pl.ds(8 * c, 8), :]
        ex = along_x(8 * c)
        ey = along_y(8 * c)
        six = f_ref[pl.ds(24 + 8 * c, 8), :]
        six += jnp.where((rows == 1) & right, pltpu.roll(ex, 7, 0), zero)
        six += jnp.where((rows == 2) & (lane < 64), pltpu.roll(ex, 1, 0), zero)
        six += jnp.where((rows == 3) & upper, pltpu.roll(ey, 7, 0), zero)
        six += jnp.where((rows == 4) & jnp.logical_not(upper), ey, zero)
        s_ref[pl.ds(24 + 8 * c, 8), :] = six
        twelve = f_ref[pl.ds(48 + 8 * c, 8), :] + jnp.where(keep, ex, zero)
        twelve += jnp.where((rows < 3) | (rows > 4) | ((rows == 3) & upper), ey, zero)
        twelve += jnp.where((rows == 4) & jnp.logical_not(upper), pltpu.roll(ey, 1, 0), zero)
        s_ref[pl.ds(48 + 8 * c, 8), :] = twelve
    small_pairs = f_ref[pl.ds(72, 8), :] * (1.0 / 27.0)
    large_pairs = (f_ref[pl.ds(80, 8), :] + along_x(24) + along_y(24)) * (1.0 / 1728.0)

    def mean(c, q):
        return s_ref[pl.ds(8 * c + q, 3, stride=24), :]

    which = lax.broadcasted_iota(jnp.int32, (3, 128), 0)
    factor = jnp.where(which == 0, 1.0 / 12.0, jnp.where(which == 1, 1.0 / 24.0, 1.0 / 48.0))
    grad = [[(mean(i, 1 + 2 * j) - mean(i, 2 + 2 * j)) * factor for j in range(3)] for i in range(3)]
    strain = [[None] * 3 for _ in range(3)]
    spin = [[None] * 3 for _ in range(3)]
    for i in range(3):
        for j in range(i, 3):
            strain[i][j] = strain[j][i] = (grad[i][j] + grad[j][i]) * 0.5
            if i != j:
                spin[i][j] = (grad[i][j] - grad[j][i]) * 0.5
                spin[j][i] = (grad[j][i] - grad[i][j]) * 0.5

    def entry(left, right, i, j):
        terms = [
            left[i][k] * right[k][j]
            for k in range(3)
            if left[i][k] is not None and right[k][j] is not None
        ]
        return sum(terms[1:], terms[0])

    magnitude = sum(
        (strain[i][j] * strain[i][j] for i in range(3) for j in range(3)),
        jnp.zeros((3, 128), jnp.float32),
    )
    columns = [strain[i][j] for i, j in INDEX_PAIRS]
    columns += [entry(strain, strain, i, j) for i, j in INDEX_PAIRS]
    columns += [entry(strain, spin, i, j) - entry(spin, strain, i, j) for i, j in INDEX_PAIRS]
    columns += [entry(spin, spin, i, j) for i, j in INDEX_PAIRS]
    columns += [magnitude * strain[i][j] for i, j in INDEX_PAIRS]
    for index, column in enumerate(columns):
        z_ref[pl.ds(index, 3, stride=30), :] = column
    z_ref[pl.ds(96, 32), :] = jnp.zeros((32, 128), jnp.float32)
    for pair, (i, j) in enumerate(INDEX_PAIRS):
        for base, box, values, width in ((90, 0, small_pairs, 3.0), (96, 48, large_pairs, 12.0)):
            first = s_ref[pl.ds(box + 8 * i, 1), :] * (1.0 / width**3)
            second = s_ref[pl.ds(box + 8 * j, 1), :] * (1.0 / width**3)
            z_ref[pl.ds(base + pair, 1), :] = values[pair : pair + 1] - first * second
    stacked = z_ref[...]
    gram_ref[...] = lax.dot_general(
        stacked[:104],
        stacked,
        (((1,), (1,)), ((), ())),
        precision=PRECISE,
        preferred_element_type=jnp.float32,
    )


def solve_kernel(total, gram_ref, z_ref, res_ref, coef_ref, p_ref):
    core = lax.axis_index("gz")
    count = 12
    rows = lax.broadcasted_iota(jnp.int32, (8, 128), 0)
    lane = lax.broadcasted_iota(jnp.int32, (8, 128), 1)
    block = []
    for i in range(count):
        value = gram_ref[pl.ds(8 * i, 8), :]
        block.append(
            jnp.where(lane == rows + 8 * i, value + 0.1 * (value + total * 1e-06), value)
        )
    for k in range(8 * count):
        at, row = k // 8, k % 8
        column = [jnp.broadcast_to(block[i][:, k : k + 1], (8, 128)) for i in range(count)]
        pivot = jnp.broadcast_to(column[at][row : row + 1, :], (8, 128))
        line = jnp.broadcast_to(block[at][row : row + 1, :], (8, 128)) / pivot
        column[at] = column[at] - (rows == row).astype(jnp.float32)
        for i in range(count):
            block[i] = block[i] - column[i] * line
    for i in range(count):
        coef_ref[pl.ds(8 * i, 8), :] = block[i][:, 96:102]
    tail = gram_ref[pl.ds(96, 8), :]
    diag = jnp.sum(jnp.where(lane == rows + 96, tail, 0.0), axis=1, keepdims=True)
    scale = jnp.sqrt(diag / total + 1e-06)
    for k in range(6):
        acc = jnp.zeros((8, 128), jnp.float32)
        for i in range(count):
            acc += jnp.broadcast_to(block[i][:, 96 + k : 97 + k], (8, 128)) * z_ref[pl.ds(8 * i, 8), :]
        p_ref[pl.ds(k, 1), :] = jnp.sum(acc, axis=0, keepdims=True)
    p_ref[pl.ds(6, 2), :] = jnp.zeros((2, 128), jnp.float32)
    residual = (z_ref[pl.ds(96, 8), :] - p_ref[...]) / jnp.broadcast_to(scale, (8, 128))
    picked = jnp.zeros((8, 128), jnp.float32)
    for place in range(4):
        even = pltpu.roll(residual, (128 - 16 * place) % 128, 1) if place else residual
        odd = pltpu.roll(residual, 112 - 16 * place, 1)
        picked = jnp.where(lane // 16 == place, jnp.where(core == 0, even, odd), picked)
    res_ref[...] = picked[:6, :64]


def moved(value, axis, step):
    size = lax.axis_size(axis)
    return lax.ppermute(value, axis, [(i, (i + step) % size) for i in range(size)])


def added_up(value, axis):
    size = lax.axis_size(axis)
    if size & (size - 1):
        return lax.psum(value, axis)
    bit = 1
    while bit < size:
        value = value + lax.ppermute(value, axis, [(i, i ^ bit) for i in range(size)])
        bit *= 2
    return value


def call(kernel, outs, scratch):
    vmem = pl.BlockSpec(memory_space=pltpu.VMEM)

    def run(*args):
        return pl.pallas_call(
            kernel,
            out_shape=[jax.ShapeDtypeStruct(shape, jnp.float32) for shape in outs],
            in_specs=[vmem] * len(args),
            out_specs=[vmem] * len(outs),
            scratch_shapes=[pltpu.VMEM(shape, jnp.float32) for shape in scratch],
        )(*args)

    return run


def chip_shards(velocity):
    bx, by, bz = velocity.shape[1:]
    length = bz * lax.axis_size("gz")
    low_type = jnp.bfloat16
    tables = [
        jnp.asarray(velocity_plane_table(bx, by), low_type),
        jnp.asarray(pair_plane_table(bx, by), low_type),
        jnp.asarray(line_table(length, 3.0, None), low_type),
        jnp.asarray(line_table(length, 6.0, None), low_type),
        jnp.asarray(line_table(length, 12.0, 6.0), low_type),
    ]
    (part,) = call(sums_kernel, [(184, 128)], [(256, 128)])(velocity, *tables)
    part = part + moved(part, "gz", 1)
    own, low, high, side = part[:88], part[88:120], part[120:152], part[152:]
    low = moved(low, "gx", -1)
    high = moved(high, "gx", 1)
    left = jnp.arange(128, dtype=jnp.int32)[None, :] < 64
    side = side + jnp.where(left, low, high)
    after = moved(side, "gy", -1)
    before = moved(side, "gy", 1)
    stacked, gram = call(features_kernel, [(128, 128), (104, 128)], [(72, 128)])(
        own, low, high, after, before
    )
    gram = added_up(added_up(gram, "gy"), "gx")
    samples = (bx // 8) * (by // 8) * (length // 8)
    total = float(samples * lax.axis_size("gx") * lax.axis_size("gy"))
    residual, coefficients = call(
        functools.partial(solve_kernel, total), [(6, 64), (96, 6)], [(8, 128)]
    )(gram, stacked)
    return (residual, coefficients)


def chip_form(mesh, velocity):
    bricks = (velocity.shape[1] // mesh.shape["gx"], velocity.shape[2] // mesh.shape["gy"])
    return mesh.shape["gz"] == 2 and bricks == (16, 16) and velocity.shape[3] == 256


def solution(mesh):
    in_specs = (P(None, "gx", "gy", "gz"),)
    out_specs = (P(None, ("gx", "gy", "gz")), P())

    def run(velocity):
        body = chip_shards if chip_form(mesh, velocity) else shards
        return jax.shard_map(
            body, mesh=mesh, in_specs=in_specs, out_specs=out_specs, check_vma=False
        )(velocity)

    return run
```

```python
import functools

import jax
import jax.numpy as jnp
import numpy as np
from jax import lax
from jax.experimental import pallas as pl
from jax.experimental.pallas import tpu as pltpu
from jax.sharding import PartitionSpec as P

PRECISE = lax.Precision.HIGHEST
INDEX_PAIRS = ((0, 0), (1, 1), (2, 2), (0, 1), (0, 2), (1, 2))
WIDTHS = (3.0, 6.0, 12.0)


def extended(block, sides, width):
    for axis, dim in sides:
        count = lax.axis_size(axis)
        forward = [(i, i + 1) for i in range(count - 1)]
        forward.append((count - 1, 0))
        backward = [(target, source) for source, target in forward]
        low = lax.ppermute(
            lax.slice_in_dim(block, block.shape[dim] - width, None, axis=dim), axis, forward
        )
        high = lax.ppermute(lax.slice_in_dim(block, 0, width, axis=dim), axis, backward)
        block = jnp.concatenate([low, block, high], axis=dim)
    return block


def window_table(combos):
    weights_table = np.zeros((len(combos), 16), np.float32)
    for row_index in range(len(combos)):
        box_width, offset = combos[row_index]
        low_edge = 7.5 + offset - box_width / 2.0
        high_edge = 7.5 + offset + box_width / 2.0
        for cell_index in range(16):
            cell_share = min(cell_index + 0.5, high_edge) - max(cell_index - 0.5, low_edge)
            weights_table[row_index, cell_index] = max(cell_share, 0.0) / box_width
    return weights_table


def velocity_combos():
    return [(box_width, offset) for box_width in WIDTHS for offset in (-2.0, 0.0, 2.0)]


def product_combos():
    return [(3.0, 0.0), (12.0, 0.0)]


def matrix_product(left_matrix, right_matrix):
    return [
        [
            left_matrix[i][0] * right_matrix[0][j]
            + left_matrix[i][1] * right_matrix[1][j]
            + left_matrix[i][2] * right_matrix[2][j]
            for j in range(3)
        ]
        for i in range(3)
    ]


def pick_pairs(matrix):
    return [matrix[i][j] for i, j in INDEX_PAIRS]


def build_rows(box_means, pair_means):
    feature_rows = []
    centre_values = []
    for width_index in range(3):
        middle = 3 * width_index + 1
        scaled = WIDTHS[width_index] ** 2 * 0.25

        def offset_value(component, direction, step_size):
            position_list = [middle, middle, middle]
            position_list[direction] = middle + step_size
            return box_means[component, position_list[0], position_list[1], position_list[2]]

        centre_values.append([box_means[i, middle, middle, middle] for i in range(3)])
        gradient = [
            [(offset_value(i, j, 1) - offset_value(i, j, -1)) * scaled for j in range(3)]
            for i in range(3)
        ]
        strain = [[(gradient[i][j] + gradient[j][i]) * 0.5 for j in range(3)] for i in range(3)]
        spin_part = [[(gradient[i][j] - gradient[j][i]) * 0.5 for j in range(3)] for i in range(3)]
        square_strain = matrix_product(strain, strain)
        first_order = matrix_product(strain, spin_part)
        second_order = matrix_product(spin_part, strain)
        commutator = [[first_order[i][j] - second_order[i][j] for j in range(3)] for i in range(3)]
        spin_square = matrix_product(spin_part, spin_part)
        magnitude = sum((strain[i][j] * strain[i][j] for i in range(3) for j in range(3)))
        feature_rows += (
            pick_pairs(strain)
            + pick_pairs(square_strain)
            + pick_pairs(commutator)
            + pick_pairs(spin_square)
        )
        feature_rows += [magnitude * entry for entry in pick_pairs(strain)]
    small_box = centre_values[0]
    large_box = centre_values[2]
    feature_rows += [
        pair_means[index, 0] - small_box[i] * small_box[j]
        for index, (i, j) in enumerate(INDEX_PAIRS)
    ]
    target_rows = [
        pair_means[index, 1] - large_box[i] * large_box[j]
        for index, (i, j) in enumerate(INDEX_PAIRS)
    ]
    return (jnp.stack(feature_rows), jnp.stack(target_rows))


def solve_fit(gram_matrix, sample_total):
    scales = jnp.sqrt(jnp.diagonal(gram_matrix) / sample_total + 1e-06)
    feature_scale = scales[:96]
    normal = gram_matrix[:96, :96] / (
        sample_total * feature_scale[:, None] * feature_scale[None, :]
    ) + 0.1 * jnp.eye(96, dtype=jnp.float32)
    target_side = gram_matrix[:96, 96:] / (sample_total * feature_scale[:, None])
    factor = jnp.linalg.cholesky(normal)
    solved = jax.scipy.linalg.cho_solve((factor, True), target_side)
    return (solved / feature_scale[:, None], scales[96:])


def axis_weights(length, weights_table):
    sample_count = length // 8
    combo_count = weights_table.shape[0]
    full_table = np.zeros((sample_count * combo_count, length + 8), np.float32)
    for sample_index in range(sample_count):
        full_table[
            sample_index * combo_count : (sample_index + 1) * combo_count,
            8 * sample_index : 8 * sample_index + 16,
        ] = weights_table
    return jnp.asarray(full_table)


def windowed(wide_field, weights_table):
    along_z = jnp.einsum(
        "cxyz,kz->cxyk",
        wide_field,
        axis_weights(wide_field.shape[3] - 8, weights_table),
        precision=PRECISE,
    )
    along_y = jnp.einsum(
        "cxyk,jy->cxjk",
        along_z,
        axis_weights(wide_field.shape[2] - 8, weights_table),
        precision=PRECISE,
    )
    return jnp.einsum(
        "cxjk,ix->cijk",
        along_y,
        axis_weights(wide_field.shape[1] - 8, weights_table),
        precision=PRECISE,
    )


def shards(velocity):
    rounded = velocity.astype(jnp.bfloat16)
    padded = extended(rounded, (("gx", 1), ("gy", 2), ("gz", 3)), 4)
    wide_field = padded.astype(jnp.float32)
    count_x = velocity.shape[1] // 8
    count_y = velocity.shape[2] // 8
    count_z = velocity.shape[3] // 8
    samples = count_x * count_y * count_z
    box_means = windowed(wide_field, window_table(velocity_combos()))
    box_means = box_means.reshape(3, count_x, 9, count_y, 9, count_z, 9)
    box_means = jnp.transpose(box_means, (0, 2, 4, 6, 1, 3, 5)).reshape(3, 9, 9, 9, samples)
    pair_field = jnp.stack([wide_field[i] * wide_field[j] for i, j in INDEX_PAIRS])
    pair_means = windowed(pair_field, window_table(product_combos())).reshape(
        6, count_x, 2, count_y, 2, count_z, 2
    )
    pair_means = jnp.stack(
        [pair_means[:, :, 0, :, 0, :, 0], pair_means[:, :, 1, :, 1, :, 1]], axis=1
    )
    pair_means = pair_means.reshape(6, 2, samples)
    features, targets = build_rows(box_means, pair_means)
    stacked = jnp.concatenate([features, targets], axis=0)
    local_gram = jnp.dot(stacked, stacked.T, precision=PRECISE, preferred_element_type=jnp.float32)
    gram_matrix = lax.psum(local_gram, ("gx", "gy", "gz"))
    sample_total = float(samples * lax.axis_size("gx") * lax.axis_size("gy") * lax.axis_size("gz"))
    coefficients, target_scale = solve_fit(gram_matrix, sample_total)
    predicted = jnp.dot(
        coefficients.T, features, precision=PRECISE, preferred_element_type=jnp.float32
    )
    residual = (targets - predicted) / target_scale[:, None]
    return (residual, coefficients)


OWN = ((0, 0), (0, 1), (1, 0), (1, 1))
FACE_LOW = ((-1, -1), (-1, 2), (-1, 0), (-1, 1))
FACE_HIGH = ((2, 0), (2, 1), (2, -1), (2, 2))
FACE_Y = ((1, -1), (1, 2), (0, -1), (0, 2))
ROWS, FACE = 48, 24


def share(centre, width, cell):
    part = min(cell + 0.5, centre + width / 2) - max(cell - 0.5, centre - width / 2)
    return max(part, 0.0)


def window(length, width, sample, difference, turns=(0,)):
    total = np.zeros(length)
    for shift, sign in ((2.0, 1.0), (-2.0, -1.0)) if difference else ((0.0, 1.0),):
        for cell in range(length):
            for turn in turns:
                total[cell] += sign * share(
                    8 * sample + 3.5 + shift, width, cell + turn * length
                )
    return total


def plane_row(bx, by, place, width, direction):
    return np.outer(
        window(bx, width, place[0], direction == 0), window(by, width, place[1], direction == 1)
    ).reshape(-1)


def velocity_plane_table(bx, by):
    none = np.zeros(bx * by)
    rows = []
    for place in OWN:
        three = [plane_row(bx, by, place, 3.0, k) for k in (0, 1, 2)]
        six = [plane_row(bx, by, place, 6.0, k) for k in (0, 1, 2)]
        rows += three + [three[2]] + six + [none]
    for places in (OWN, FACE_LOW, FACE_HIGH, FACE_Y):
        for place in places:
            twelve = [plane_row(bx, by, place, 12.0, k) for k in (0, 1, 2)]
            along = {FACE_LOW: 0, FACE_HIGH: 0, FACE_Y: 1}.get(places)
            last = none if along is None else plane_row(bx, by, place, 6.0, along)
            rows += twelve + [twelve[2], last, none, none, none]
    return np.stack(rows)


def pair_plane_table(bx, by):
    rows = [plane_row(bx, by, place, 3.0, 2) for place in OWN]
    for places in (OWN, FACE_LOW, FACE_HIGH, FACE_Y):
        rows += [plane_row(bx, by, place, 12.0, 2) for place in places]
    while len(rows) % 16:
        rows.append(np.zeros(bx * by))
    return np.stack(rows)


def line_table(length, blocks):
    columns = []
    for width, difference in blocks:
        for sample in range(length // 8):
            if width:
                columns.append(window(length, width, sample, difference, (-1, 0, 1)))
            else:
                columns.append(np.zeros(length))
    return np.stack(columns, axis=1)


def three_parts(value):
    high = value.astype(jnp.bfloat16)
    rest = value - high.astype(jnp.float32)
    middle = rest.astype(jnp.bfloat16)
    low = (rest - middle.astype(jnp.float32)).astype(jnp.bfloat16)
    return high, middle, low


def mxu(left, right):
    return jnp.dot(left, right, preferred_element_type=jnp.float32)


def sums_kernel(x_hbm, wv_hbm, wp_hbm, la_hbm, lb_hbm, out_ref, x_ref, wv, wp, la, lb, pair_ref, sems):
    core = lax.axis_index("gz")
    cells = x_ref.shape[1] * x_ref.shape[2]
    length = x_ref.shape[3]
    begin = pl.multiple_of(core * length, length)
    copies = [pltpu.make_async_copy(wv_hbm, wv, sems.at[0])]
    copies += [pltpu.make_async_copy(x_hbm.at[c], x_ref.at[c], sems.at[1 + c]) for c in range(3)]
    copies += [pltpu.make_async_copy(wp_hbm, wp, sems.at[4])]
    copies += [pltpu.make_async_copy(la_hbm.at[pl.ds(begin, length)], la, sems.at[5])]
    copies += [pltpu.make_async_copy(lb_hbm.at[pl.ds(begin, length)], lb, sems.at[6])]
    for copy in copies:
        copy.start()
    rows = lax.broadcasted_iota(jnp.int32, (8, 128), 0)
    lanes = lax.broadcasted_iota(jnp.int32, (8, 128), 1) // 32
    pair_ref[...] = jnp.zeros(pair_ref.shape, jnp.float32)

    def gathered(groups, blocks):
        total = jnp.zeros((8, 128), jnp.float32)
        for place in range(4):
            base = merged = groups[8 * place : 8 * place + 8]
            for block, chosen in blocks:
                hit = rows == chosen[0]
                for row in chosen[1:]:
                    hit = hit | (rows == row)
                merged = jnp.where(hit, pltpu.roll(base, 128 - 32 * block, 1), merged)
            if place:
                merged = pltpu.roll(merged, 32 * place, 1)
            total = jnp.where(lanes == place, merged, total)
        return total

    for copy in copies:
        copy.wait()
    fields = [x_ref[c].reshape(cells, length).astype(jnp.bfloat16) for c in range(3)]
    planes = [mxu(wv[...], field) for field in fields]
    wide = [field.astype(jnp.float32) for field in fields]
    count = wp.shape[0]
    weights = jnp.concatenate([wp[...], wp[...]], axis=1)
    for pair, (i, j) in enumerate(INDEX_PAIRS):
        product = wide[i] * wide[j]
        high = product.astype(jnp.bfloat16)
        low = (product - high.astype(jnp.float32)).astype(jnp.bfloat16)
        pair_ref[pl.ds(pair, count, stride=8), :] = mxu(
            weights, jnp.concatenate([high, low], axis=0)
        )

    def along_line(value, line):
        high, middle, low = three_parts(value)
        return mxu(
            jnp.concatenate([high, middle], axis=1), jnp.concatenate([line, line], axis=0)
        ) + mxu(low, line)

    narrow = along_line(
        jnp.concatenate([plane[:32] for plane in planes] + [pair_ref[pl.ds(0, 32), :]], axis=0),
        la[...],
    )
    broad = along_line(
        jnp.concatenate([plane[32:] for plane in planes] + [pair_ref[pl.ds(32, 128), :]], axis=0),
        lb[...],
    )
    for c in range(3):
        value = gathered(narrow[32 * c : 32 * c + 32], ((1, (2,)), (2, (4, 5)), (3, (6,))))
        out_ref[pl.ds(27 + 3 * c, 3), :] = value[0:3]
        out_ref[pl.ds(36 + c, 1), :] = value[3:4]
        out_ref[pl.ds(12 + c, 1), :] = value[4:5]
        out_ref[pl.ds(21 + c, 1), :] = value[5:6]
        out_ref[pl.ds(24 + c, 1), :] = value[6:7]
        for part in range(4):
            at = 128 * c + 32 * part
            base = (0, ROWS + FACE, ROWS + 2 * FACE, ROWS)[part]
            blocks = ((1, (2,)), (2, (4,))) if part else ((1, (2,)),)
            value = gathered(broad[at : at + 32], blocks)
            out_ref[pl.ds(base + 3 * c, 3), :] = value[0:3]
            out_ref[pl.ds(base + 9 + c, 1), :] = value[3:4]
            if part:
                live, still = (12, 21) if part < 3 else (21, 12)
                out_ref[pl.ds(base + live + c, 1), :] = value[4:5]
                out_ref[pl.ds(base + still + c, 1), :] = jnp.zeros((1, 128), jnp.float32)
    out_ref[pl.ds(39, 6), :] = gathered(narrow[96:128], ())[:6]
    out_ref[pl.ds(45, 3), :] = jnp.zeros((3, 128), jnp.float32)
    for part in range(4):
        base = (0, ROWS + FACE, ROWS + 2 * FACE, ROWS)[part]
        out_ref[pl.ds(base + 15, 6), :] = gathered(broad[384 + 32 * part : 416 + 32 * part], ())[:6]


def features_kernel(near_ref, far_ref, z_out, gram_ref, b_ref, a_ref, z_ref):
    core = lax.axis_index("gz")
    mine = lax.axis_index("gy")
    chips = b_ref.shape[0]
    for slot in range(chips):
        swapped = (slot % 2) * 2 + slot // 2
        at = jnp.bitwise_xor(mine, jnp.where(core == 0, slot, swapped))
        b_ref[at] = near_ref[slot] if slot < 2 else far_ref[slot - 2]
    lane = lax.broadcasted_iota(jnp.int32, (FACE, 128), 1)
    upper = (lane // 32) % 2 == 1
    z_ref[:, 96:, :] = jnp.zeros((chips, 32, 128), jnp.float32)
    for chip in range(chips):
        after = pltpu.roll(b_ref[(chip + 1) % chips, ROWS:, :], 96, 1)
        before = pltpu.roll(b_ref[(chip - 1) % chips, ROWS:, :], 32, 1)
        sums = b_ref[chip, :FACE, :] + jnp.where(upper, after, before)
        base = 27 * chip
        a_ref[pl.ds(base, 9), :] = b_ref[chip, 27:36, :]
        a_ref[pl.ds(base + 9, 3, stride=3), :] = sums[12:15]
        a_ref[pl.ds(base + 10, 3, stride=3), :] = sums[21:24]
        a_ref[pl.ds(base + 11, 3, stride=3), :] = b_ref[chip, 24:27, :]
        a_ref[pl.ds(base + 18, 9), :] = sums[0:9]
        for at, centres, products, width in (
            (90, b_ref[chip, 36:39, :], b_ref[chip, 39:45, :], 3.0),
            (96, sums[9:12], sums[15:21], 12.0),
        ):
            means = [centres[c : c + 1] * (1.0 / width**3) for c in range(3)]
            for pair, (i, j) in enumerate(INDEX_PAIRS):
                z_ref[chip, pl.ds(at + pair, 1), :] = (
                    products[pair : pair + 1] * (1.0 / width**3) - means[i] * means[j]
                )
    total = 3 * chips
    width = lax.broadcasted_iota(jnp.int32, (total, 128), 0) % 3
    factor = jnp.where(width == 0, 1.0 / 12.0, jnp.where(width == 1, 1.0 / 24.0, 1.0 / 48.0))
    grad = [
        [a_ref[pl.ds(3 * i + j, total, stride=9), :] * factor for j in range(3)] for i in range(3)
    ]
    strain = [[None] * 3 for _ in range(3)]
    spin = [[None] * 3 for _ in range(3)]
    for i in range(3):
        for j in range(i, 3):
            strain[i][j] = strain[j][i] = (grad[i][j] + grad[j][i]) * 0.5
            if i != j:
                spin[i][j] = (grad[i][j] - grad[j][i]) * 0.5
                spin[j][i] = (grad[j][i] - grad[i][j]) * 0.5

    def entry(left, right, i, j):
        terms = [
            left[i][k] * right[k][j]
            for k in range(3)
            if left[i][k] is not None and right[k][j] is not None
        ]
        return sum(terms[1:], terms[0])

    squares = [strain[i][j] * strain[i][j] for i in range(3) for j in range(3)]
    magnitude = sum(squares[1:], squares[0])
    columns = [strain[i][j] for i, j in INDEX_PAIRS]
    columns += [entry(strain, strain, i, j) for i, j in INDEX_PAIRS]
    columns += [entry(strain, spin, i, j) - entry(spin, strain, i, j) for i, j in INDEX_PAIRS]
    columns += [entry(spin, spin, i, j) for i, j in INDEX_PAIRS]
    columns += [magnitude * strain[i][j] for i, j in INDEX_PAIRS]
    for index, column in enumerate(columns):
        for chip in range(chips):
            z_ref[chip, pl.ds(index, 3, stride=30), :] = column[3 * chip : 3 * chip + 3]
    z_out[...] = z_ref[mine]
    stacked = jnp.concatenate([z_ref[chip] for chip in range(chips)], axis=1)
    gram_ref[...] = lax.dot_general(
        stacked[:104],
        stacked,
        (((1,), (1,)), ((), ())),
        precision=PRECISE,
        preferred_element_type=jnp.float32,
    )


def solve_kernel(total, gram_ref, z_ref, res_ref, coef_ref):
    core = lax.axis_index("gz")
    one = jnp.where(core >= 0, 1.0, 2.0)
    count, group = 12, 2
    rows = lax.broadcasted_iota(jnp.int32, (8, 128), 0)
    lane = lax.broadcasted_iota(jnp.int32, (8, 128), 1)
    block = []
    for i in range(count + 1):
        value = gram_ref[pl.ds(8 * i, 8), :]
        if i < count:
            ridge = value + 0.1 * (value + total * 1e-06)
            value = jnp.where(lane == rows + 8 * i, ridge, value)
        block.append(value)
    diag = jnp.sum(jnp.where(lane == rows + 96, block[count], 0.0), axis=1, keepdims=True)
    scale = jnp.broadcast_to(jnp.sqrt(diag / total + 1e-06), (8, 128))

    def spread(value, column):
        return jnp.broadcast_to(value[:, column : column + 1], (8, 128))

    def row_of(parts, row):
        return jnp.broadcast_to(parts[row // 8][row % 8 : row % 8 + 1, :], (8, 128))

    for start in range(0, count, group):
        size = 8 * group
        first = 8 * start
        square = [
            [spread(block[start + p], first + m) * one for p in range(group)] for m in range(size)
        ]
        below = {
            i: [spread(block[i], first + m) for m in range(size)]
            for i in range(start + group, count + 1)
        }
        panel = []
        for p in range(group):
            unit = (lane == rows + first + 8 * p).astype(jnp.float32)
            inside = (lane >= first) & (lane < first + size)
            panel.append(jnp.where(inside, -unit, block[start + p]))
        inverses = []
        for m in range(size):
            inverses.append(1.0 / row_of(square[m], m))
            factor = [
                jnp.where(rows == m - 8 * p, 0.0, square[m][p]) if m // 8 == p else square[m][p]
                for p in range(group)
            ]
            for k in range(m + 1, size):
                line = row_of(square[k], m) * inverses[m]
                square[k] = [square[k][p] - factor[p] * line for p in range(group)]
            line = row_of(panel, m) * inverses[m]
            panel = [panel[p] - factor[p] * line for p in range(group)]
        lines = [row_of(panel, m) * inverses[m] for m in range(size)]
        for i in below:
            terms = [below[i][m] * lines[m] for m in range(size)]
            while len(terms) > 1:
                terms = [terms[t] + terms[t + 1] for t in range(0, len(terms), 2)]
            outside = (lane < first) | (lane >= first + size)
            block[i] = jnp.where(outside, block[i], 0.0) - terms[0]
    answer = jnp.where(lane < 96, block[count], 0.0)
    coef_ref[...] = answer[:6, :96]
    predicted = jnp.dot(answer, z_ref[...], precision=PRECISE, preferred_element_type=jnp.float32)
    residual = (z_ref[pl.ds(96, 8), :] - predicted) / scale
    picked = jnp.zeros((8, 128), jnp.float32)
    for place in range(4):
        even = pltpu.roll(residual, (128 - 16 * place) % 128, 1) if place else residual
        odd = pltpu.roll(residual, 112 - 16 * place, 1)
        picked = jnp.where(lane // 16 == place, jnp.where(core == 0, even, odd), picked)
    res_ref[...] = picked[:6, :64]


def moved(value, axis, step):
    size = lax.axis_size(axis)
    return lax.ppermute(value, axis, [(i, (i + step) % size) for i in range(size)])


def added_up(value, axis):
    size = lax.axis_size(axis)
    bit = 1
    while bit < size:
        value = value + lax.ppermute(value, axis, [(i, i ^ bit) for i in range(size)])
        bit *= 2
    return value


def call(kernel, outs, scratch, place=pltpu.VMEM):
    def run(*args):
        return pl.pallas_call(
            kernel,
            out_shape=[jax.ShapeDtypeStruct(shape, jnp.float32) for shape in outs],
            in_specs=[pl.BlockSpec(memory_space=place)] * len(args),
            out_specs=[pl.BlockSpec(memory_space=pltpu.VMEM)] * len(outs),
            scratch_shapes=scratch,
            compiler_params=pltpu.CompilerParams(vmem_limit_bytes=8 * 2**20),
        )(*args)

    return run


def chip_shards(velocity):
    bx, by, bz = velocity.shape[1:]
    chips = lax.axis_size("gy")
    length = bz * lax.axis_size("gz")
    low_type, wide_type = jnp.bfloat16, jnp.float32
    tables = [
        velocity_plane_table(bx, by),
        pair_plane_table(bx, by),
        line_table(length, ((3.0, False), (3.0, True), (6.0, False), (6.0, True))),
        line_table(length, ((12.0, False), (12.0, True), (6.0, False), (0.0, False))),
    ]
    tables = [jnp.asarray(table, low_type) for table in tables]
    shapes = [tables[0].shape, tables[1].shape, (bz, 128), (bz, 128)]
    (part,) = call(
        sums_kernel,
        [(ROWS + 3 * FACE, 128)],
        [pltpu.VMEM(velocity.shape, wide_type)]
        + [pltpu.VMEM(shape, low_type) for shape in shapes]
        + [pltpu.VMEM((8 * shapes[1][0], 128), wide_type), pltpu.SemaphoreType.DMA((7,))],
        pltpu.HBM,
    )(velocity, *tables)
    part = part + moved(part, "gz", 1)
    own = part[: ROWS + FACE]
    low = moved(part[ROWS + FACE : ROWS + 2 * FACE], "gx", -1)
    high = moved(part[ROWS + 2 * FACE :], "gx", 1)
    left = jnp.arange(128, dtype=jnp.int32)[None, :] < 64
    middle = jnp.zeros((ROWS - FACE, 128), wide_type)
    own = own + jnp.concatenate(
        [jnp.where(left, high, low), middle, jnp.where(left, low, high)], axis=0
    )

    def across(value, bits):
        pairs = []
        for chip in range(chips):
            for core in range(2):
                pairs.append((2 * chip + core, 2 * (chip ^ bits[core]) + core))
        return lax.ppermute(value, ("gy", "gz"), pairs)

    near = jnp.stack([own, across(own, (1, 2))])
    far = across(near, (2, 1))
    stacked, gram = call(
        features_kernel,
        [(128, 128), (104, 128)],
        [
            pltpu.VMEM((chips, ROWS + FACE, 128), wide_type),
            pltpu.VMEM((27 * chips, 128), wide_type),
            pltpu.VMEM((chips, 128, 128), wide_type),
        ],
    )(near, far)
    gram = added_up(gram, "gx")
    samples = (bx // 8) * (by // 8) * (length // 8)
    total = float(samples * lax.axis_size("gx") * chips)
    residual, coefficients = call(
        functools.partial(solve_kernel, total), [(6, 64), (6, 96)], []
    )(gram, stacked)
    return (residual, coefficients.T)


def chip_form(mesh, velocity):
    shape = mesh.shape
    brick = (velocity.shape[1] // shape["gx"], velocity.shape[2] // shape["gy"])
    even = shape["gx"] & (shape["gx"] - 1) == 0
    return (
        even and shape["gy"] == 4 and shape["gz"] == 2
        and brick == (16, 16) and velocity.shape[3] == 256
    )


def solution(mesh):
    in_specs = (P(None, "gx", "gy", "gz"),)
    out_specs = (P(None, ("gx", "gy", "gz")), P())

    def run(velocity):
        body = chip_shards if chip_form(mesh, velocity) else shards
        return jax.shard_map(
            body, mesh=mesh, in_specs=in_specs, out_specs=out_specs, check_vma=False
        )(velocity)

    return run
```

```python
import functools

import jax
import jax.numpy as jnp
import numpy as np
from jax import lax
from jax.experimental import pallas as pl
from jax.experimental.pallas import tpu as pltpu
from jax.sharding import PartitionSpec as P

PRECISE = lax.Precision.HIGHEST
INDEX_PAIRS = ((0, 0), (1, 1), (2, 2), (0, 1), (0, 2), (1, 2))
WIDTHS = (3.0, 6.0, 12.0)


def extended(block, sides, width):
    for axis, dim in sides:
        count = lax.axis_size(axis)
        forward = [(i, i + 1) for i in range(count - 1)]
        forward.append((count - 1, 0))
        backward = [(target, source) for source, target in forward]
        low = lax.ppermute(
            lax.slice_in_dim(block, block.shape[dim] - width, None, axis=dim), axis, forward
        )
        high = lax.ppermute(lax.slice_in_dim(block, 0, width, axis=dim), axis, backward)
        block = jnp.concatenate([low, block, high], axis=dim)
    return block


def window_table(combos):
    weights_table = np.zeros((len(combos), 16), np.float32)
    for row_index in range(len(combos)):
        box_width, offset = combos[row_index]
        low_edge = 7.5 + offset - box_width / 2.0
        high_edge = 7.5 + offset + box_width / 2.0
        for cell_index in range(16):
            cell_share = min(cell_index + 0.5, high_edge) - max(cell_index - 0.5, low_edge)
            weights_table[row_index, cell_index] = max(cell_share, 0.0) / box_width
    return weights_table


def velocity_combos():
    return [(box_width, offset) for box_width in WIDTHS for offset in (-2.0, 0.0, 2.0)]


def product_combos():
    return [(3.0, 0.0), (12.0, 0.0)]


def matrix_product(left_matrix, right_matrix):
    return [
        [
            left_matrix[i][0] * right_matrix[0][j]
            + left_matrix[i][1] * right_matrix[1][j]
            + left_matrix[i][2] * right_matrix[2][j]
            for j in range(3)
        ]
        for i in range(3)
    ]


def pick_pairs(matrix):
    return [matrix[i][j] for i, j in INDEX_PAIRS]


def build_rows(box_means, pair_means):
    feature_rows = []
    centre_values = []
    for width_index in range(3):
        middle = 3 * width_index + 1
        scaled = WIDTHS[width_index] ** 2 * 0.25

        def offset_value(component, direction, step_size):
            position_list = [middle, middle, middle]
            position_list[direction] = middle + step_size
            return box_means[component, position_list[0], position_list[1], position_list[2]]

        centre_values.append([box_means[i, middle, middle, middle] for i in range(3)])
        gradient = [
            [(offset_value(i, j, 1) - offset_value(i, j, -1)) * scaled for j in range(3)]
            for i in range(3)
        ]
        strain = [[(gradient[i][j] + gradient[j][i]) * 0.5 for j in range(3)] for i in range(3)]
        spin_part = [[(gradient[i][j] - gradient[j][i]) * 0.5 for j in range(3)] for i in range(3)]
        square_strain = matrix_product(strain, strain)
        first_order = matrix_product(strain, spin_part)
        second_order = matrix_product(spin_part, strain)
        commutator = [[first_order[i][j] - second_order[i][j] for j in range(3)] for i in range(3)]
        spin_square = matrix_product(spin_part, spin_part)
        magnitude = sum((strain[i][j] * strain[i][j] for i in range(3) for j in range(3)))
        feature_rows += (
            pick_pairs(strain)
            + pick_pairs(square_strain)
            + pick_pairs(commutator)
            + pick_pairs(spin_square)
        )
        feature_rows += [magnitude * entry for entry in pick_pairs(strain)]
    small_box = centre_values[0]
    large_box = centre_values[2]
    feature_rows += [
        pair_means[index, 0] - small_box[i] * small_box[j]
        for index, (i, j) in enumerate(INDEX_PAIRS)
    ]
    target_rows = [
        pair_means[index, 1] - large_box[i] * large_box[j]
        for index, (i, j) in enumerate(INDEX_PAIRS)
    ]
    return (jnp.stack(feature_rows), jnp.stack(target_rows))


def solve_fit(gram_matrix, sample_total):
    scales = jnp.sqrt(jnp.diagonal(gram_matrix) / sample_total + 1e-06)
    feature_scale = scales[:96]
    normal = gram_matrix[:96, :96] / (
        sample_total * feature_scale[:, None] * feature_scale[None, :]
    ) + 0.1 * jnp.eye(96, dtype=jnp.float32)
    target_side = gram_matrix[:96, 96:] / (sample_total * feature_scale[:, None])
    factor = jnp.linalg.cholesky(normal)
    solved = jax.scipy.linalg.cho_solve((factor, True), target_side)
    return (solved / feature_scale[:, None], scales[96:])


def axis_weights(length, weights_table):
    sample_count = length // 8
    combo_count = weights_table.shape[0]
    full_table = np.zeros((sample_count * combo_count, length + 8), np.float32)
    for sample_index in range(sample_count):
        full_table[
            sample_index * combo_count : (sample_index + 1) * combo_count,
            8 * sample_index : 8 * sample_index + 16,
        ] = weights_table
    return jnp.asarray(full_table)


def windowed(wide_field, weights_table):
    along_z = jnp.einsum(
        "cxyz,kz->cxyk",
        wide_field,
        axis_weights(wide_field.shape[3] - 8, weights_table),
        precision=PRECISE,
    )
    along_y = jnp.einsum(
        "cxyk,jy->cxjk",
        along_z,
        axis_weights(wide_field.shape[2] - 8, weights_table),
        precision=PRECISE,
    )
    return jnp.einsum(
        "cxjk,ix->cijk",
        along_y,
        axis_weights(wide_field.shape[1] - 8, weights_table),
        precision=PRECISE,
    )


def shards(velocity):
    rounded = velocity.astype(jnp.bfloat16)
    padded = extended(rounded, (("gx", 1), ("gy", 2), ("gz", 3)), 4)
    wide_field = padded.astype(jnp.float32)
    count_x = velocity.shape[1] // 8
    count_y = velocity.shape[2] // 8
    count_z = velocity.shape[3] // 8
    samples = count_x * count_y * count_z
    box_means = windowed(wide_field, window_table(velocity_combos()))
    box_means = box_means.reshape(3, count_x, 9, count_y, 9, count_z, 9)
    box_means = jnp.transpose(box_means, (0, 2, 4, 6, 1, 3, 5)).reshape(3, 9, 9, 9, samples)
    pair_field = jnp.stack([wide_field[i] * wide_field[j] for i, j in INDEX_PAIRS])
    pair_means = windowed(pair_field, window_table(product_combos())).reshape(
        6, count_x, 2, count_y, 2, count_z, 2
    )
    pair_means = jnp.stack(
        [pair_means[:, :, 0, :, 0, :, 0], pair_means[:, :, 1, :, 1, :, 1]], axis=1
    )
    pair_means = pair_means.reshape(6, 2, samples)
    features, targets = build_rows(box_means, pair_means)
    stacked = jnp.concatenate([features, targets], axis=0)
    local_gram = jnp.dot(stacked, stacked.T, precision=PRECISE, preferred_element_type=jnp.float32)
    gram_matrix = lax.psum(local_gram, ("gx", "gy", "gz"))
    sample_total = float(samples * lax.axis_size("gx") * lax.axis_size("gy") * lax.axis_size("gz"))
    coefficients, target_scale = solve_fit(gram_matrix, sample_total)
    predicted = jnp.dot(
        coefficients.T, features, precision=PRECISE, preferred_element_type=jnp.float32
    )
    residual = (targets - predicted) / target_scale[:, None]
    return (residual, coefficients)


OWN = ((0, 0), (0, 1), (1, 0), (1, 1))
FACE_LOW = ((-1, -1), (-1, 2), (-1, 0), (-1, 1))
FACE_HIGH = ((2, 0), (2, 1), (2, -1), (2, 2))
FACE_Y = ((1, -1), (1, 2), (0, -1), (0, 2))
ROWS, FACE = 48, 24


def share(centre, width, cell):
    part = min(cell + 0.5, centre + width / 2) - max(cell - 0.5, centre - width / 2)
    return max(part, 0.0)


def window(length, width, sample, difference, turns=(0,)):
    total = np.zeros(length)
    for shift, sign in ((2.0, 1.0), (-2.0, -1.0)) if difference else ((0.0, 1.0),):
        for cell in range(length):
            for turn in turns:
                total[cell] += sign * share(
                    8 * sample + 3.5 + shift, width, cell + turn * length
                )
    return total


def plane_row(bx, by, place, width, direction):
    return np.outer(
        window(bx, width, place[0], direction == 0), window(by, width, place[1], direction == 1)
    ).reshape(-1)


def velocity_plane_table(bx, by):
    none = np.zeros(bx * by)
    rows = []
    for place in OWN:
        three = [plane_row(bx, by, place, 3.0, k) for k in (0, 1, 2)]
        six = [plane_row(bx, by, place, 6.0, k) for k in (0, 1, 2)]
        rows += three + [three[2]] + six + [none]
    for places in (OWN, FACE_LOW, FACE_HIGH, FACE_Y):
        for place in places:
            twelve = [plane_row(bx, by, place, 12.0, k) for k in (0, 1, 2)]
            along = {FACE_LOW: 0, FACE_HIGH: 0, FACE_Y: 1}.get(places)
            last = none if along is None else plane_row(bx, by, place, 6.0, along)
            rows += twelve + [twelve[2], last, none, none, none]
    return np.stack(rows)


def pair_plane_table(bx, by):
    rows = [plane_row(bx, by, place, 3.0, 2) for place in OWN]
    for places in (OWN, FACE_LOW, FACE_HIGH, FACE_Y):
        rows += [plane_row(bx, by, place, 12.0, 2) for place in places]
    while len(rows) % 16:
        rows.append(np.zeros(bx * by))
    return np.stack(rows)


def line_table(length, blocks):
    columns = []
    for width, difference in blocks:
        for sample in range(length // 8):
            if width:
                columns.append(window(length, width, sample, difference, (-1, 0, 1)))
            else:
                columns.append(np.zeros(length))
    return np.stack(columns, axis=1)


def three_parts(value):
    high = value.astype(jnp.bfloat16)
    rest = value - high.astype(jnp.float32)
    middle = rest.astype(jnp.bfloat16)
    low = (rest - middle.astype(jnp.float32)).astype(jnp.bfloat16)
    return high, middle, low


def mxu(left, right):
    return jnp.dot(left, right, preferred_element_type=jnp.float32)


def sums_kernel(x_hbm, wv_hbm, wp_hbm, la_hbm, lb_hbm, out_ref, x_ref, wv, wp, la, lb, pair_ref, sems):
    core = lax.axis_index("gz")
    cells = x_ref.shape[1] * x_ref.shape[2]
    length = x_ref.shape[3]
    begin = pl.multiple_of(core * length, length)
    copies = [pltpu.make_async_copy(wv_hbm, wv, sems.at[0])]
    copies += [pltpu.make_async_copy(x_hbm.at[c], x_ref.at[c], sems.at[1 + c]) for c in range(3)]
    copies += [pltpu.make_async_copy(wp_hbm, wp, sems.at[4])]
    copies += [pltpu.make_async_copy(la_hbm.at[pl.ds(begin, length)], la, sems.at[5])]
    copies += [pltpu.make_async_copy(lb_hbm.at[pl.ds(begin, length)], lb, sems.at[6])]
    for copy in copies:
        copy.start()
    rows = lax.broadcasted_iota(jnp.int32, (8, 128), 0)
    lanes = lax.broadcasted_iota(jnp.int32, (8, 128), 1) // 32
    pair_ref[...] = jnp.zeros(pair_ref.shape, jnp.float32)

    def gathered(groups, blocks):
        total = jnp.zeros((8, 128), jnp.float32)
        for place in range(4):
            base = merged = groups[8 * place : 8 * place + 8]
            for block, chosen in blocks:
                hit = rows == chosen[0]
                for row in chosen[1:]:
                    hit = hit | (rows == row)
                merged = jnp.where(hit, pltpu.roll(base, 128 - 32 * block, 1), merged)
            if place:
                merged = pltpu.roll(merged, 32 * place, 1)
            total = jnp.where(lanes == place, merged, total)
        return total

    for copy in copies:
        copy.wait()
    fields = [x_ref[c].reshape(cells, length).astype(jnp.bfloat16) for c in range(3)]
    planes = [mxu(wv[...], field) for field in fields]
    wide = [field.astype(jnp.float32) for field in fields]
    count = wp.shape[0]
    weights = jnp.concatenate([wp[...], wp[...]], axis=1)
    for pair, (i, j) in enumerate(INDEX_PAIRS):
        product = wide[i] * wide[j]
        high = product.astype(jnp.bfloat16)
        low = (product - high.astype(jnp.float32)).astype(jnp.bfloat16)
        pair_ref[pl.ds(pair, count, stride=8), :] = mxu(
            weights, jnp.concatenate([high, low], axis=0)
        )

    def along_line(value, line):
        high, middle, low = three_parts(value)
        return mxu(
            jnp.concatenate([high, middle], axis=1), jnp.concatenate([line, line], axis=0)
        ) + mxu(low, line)

    narrow = along_line(
        jnp.concatenate([plane[:32] for plane in planes] + [pair_ref[pl.ds(0, 32), :]], axis=0),
        la[...],
    )
    broad = along_line(
        jnp.concatenate([plane[32:] for plane in planes] + [pair_ref[pl.ds(32, 128), :]], axis=0),
        lb[...],
    )
    for c in range(3):
        value = gathered(narrow[32 * c : 32 * c + 32], ((1, (2,)), (2, (4, 5)), (3, (6,))))
        out_ref[pl.ds(27 + 3 * c, 3), :] = value[0:3]
        out_ref[pl.ds(36 + c, 1), :] = value[3:4]
        out_ref[pl.ds(12 + c, 1), :] = value[4:5]
        out_ref[pl.ds(21 + c, 1), :] = value[5:6]
        out_ref[pl.ds(24 + c, 1), :] = value[6:7]
        for part in range(4):
            at = 128 * c + 32 * part
            base = (0, ROWS + FACE, ROWS + 2 * FACE, ROWS)[part]
            blocks = ((1, (2,)), (2, (4,))) if part else ((1, (2,)),)
            value = gathered(broad[at : at + 32], blocks)
            out_ref[pl.ds(base + 3 * c, 3), :] = value[0:3]
            out_ref[pl.ds(base + 9 + c, 1), :] = value[3:4]
            if part:
                live, still = (12, 21) if part < 3 else (21, 12)
                out_ref[pl.ds(base + live + c, 1), :] = value[4:5]
                out_ref[pl.ds(base + still + c, 1), :] = jnp.zeros((1, 128), jnp.float32)
    out_ref[pl.ds(39, 6), :] = gathered(narrow[96:128], ())[:6]
    out_ref[pl.ds(45, 3), :] = jnp.zeros((3, 128), jnp.float32)
    for part in range(4):
        base = (0, ROWS + FACE, ROWS + 2 * FACE, ROWS)[part]
        out_ref[pl.ds(base + 15, 6), :] = gathered(broad[384 + 32 * part : 416 + 32 * part], ())[:6]


def features_kernel(near_ref, far_ref, z_out, gram_ref, b_ref, a_ref, z_ref):
    mine = lax.axis_index("gy")
    chips = b_ref.shape[0]
    for slot in range(chips):
        b_ref[jnp.bitwise_xor(mine, slot)] = near_ref[slot] if slot < 2 else far_ref[slot - 2]
    lane = lax.broadcasted_iota(jnp.int32, (FACE, 128), 1)
    upper = (lane // 32) % 2 == 1
    z_ref[:, 96:, :] = jnp.zeros((chips, 32, 128), jnp.float32)
    for chip in range(chips):
        after = pltpu.roll(b_ref[(chip + 1) % chips, ROWS:, :], 96, 1)
        before = pltpu.roll(b_ref[(chip - 1) % chips, ROWS:, :], 32, 1)
        sums = b_ref[chip, :FACE, :] + jnp.where(upper, after, before)
        base = 27 * chip
        a_ref[pl.ds(base, 9), :] = b_ref[chip, 27:36, :]
        a_ref[pl.ds(base + 9, 3, stride=3), :] = sums[12:15]
        a_ref[pl.ds(base + 10, 3, stride=3), :] = sums[21:24]
        a_ref[pl.ds(base + 11, 3, stride=3), :] = b_ref[chip, 24:27, :]
        a_ref[pl.ds(base + 18, 9), :] = sums[0:9]
        for at, centres, products, width in (
            (90, b_ref[chip, 36:39, :], b_ref[chip, 39:45, :], 3.0),
            (96, sums[9:12], sums[15:21], 12.0),
        ):
            means = [centres[c : c + 1] * (1.0 / width**3) for c in range(3)]
            for pair, (i, j) in enumerate(INDEX_PAIRS):
                z_ref[chip, pl.ds(at + pair, 1), :] = (
                    products[pair : pair + 1] * (1.0 / width**3) - means[i] * means[j]
                )
    total = 3 * chips
    width = lax.broadcasted_iota(jnp.int32, (total, 128), 0) % 3
    factor = jnp.where(width == 0, 1.0 / 12.0, jnp.where(width == 1, 1.0 / 24.0, 1.0 / 48.0))
    grad = [
        [a_ref[pl.ds(3 * i + j, total, stride=9), :] * factor for j in range(3)] for i in range(3)
    ]
    strain = [[None] * 3 for _ in range(3)]
    spin = [[None] * 3 for _ in range(3)]
    for i in range(3):
        for j in range(i, 3):
            strain[i][j] = strain[j][i] = (grad[i][j] + grad[j][i]) * 0.5
            if i != j:
                spin[i][j] = (grad[i][j] - grad[j][i]) * 0.5
                spin[j][i] = (grad[j][i] - grad[i][j]) * 0.5

    def entry(left, right, i, j):
        terms = [
            left[i][k] * right[k][j]
            for k in range(3)
            if left[i][k] is not None and right[k][j] is not None
        ]
        return sum(terms[1:], terms[0])

    squares = [strain[i][j] * strain[i][j] for i in range(3) for j in range(3)]
    magnitude = sum(squares[1:], squares[0])
    columns = [strain[i][j] for i, j in INDEX_PAIRS]
    columns += [entry(strain, strain, i, j) for i, j in INDEX_PAIRS]
    columns += [entry(strain, spin, i, j) - entry(spin, strain, i, j) for i, j in INDEX_PAIRS]
    columns += [entry(spin, spin, i, j) for i, j in INDEX_PAIRS]
    columns += [magnitude * strain[i][j] for i, j in INDEX_PAIRS]
    for index, column in enumerate(columns):
        for chip in range(chips):
            z_ref[chip, pl.ds(index, 3, stride=30), :] = column[3 * chip : 3 * chip + 3]
    z_out[...] = z_ref[mine]
    stacked = jnp.concatenate([z_ref[chip] for chip in range(chips)], axis=1)
    gram_ref[...] = lax.dot_general(
        stacked[:104],
        stacked,
        (((1,), (1,)), ((), ())),
        precision=PRECISE,
        preferred_element_type=jnp.float32,
    )


def solve_kernel(total, gram_ref, z_ref, res_ref, coef_ref):
    core = lax.axis_index("gz")
    one = jnp.where(core >= 0, 1.0, 2.0)
    count, group = 12, 2
    rows = lax.broadcasted_iota(jnp.int32, (8, 128), 0)
    lane = lax.broadcasted_iota(jnp.int32, (8, 128), 1)
    block = []
    for i in range(count + 1):
        value = gram_ref[pl.ds(8 * i, 8), :]
        if i < count:
            ridge = value + 0.1 * (value + total * 1e-06)
            value = jnp.where(lane == rows + 8 * i, ridge, value)
        block.append(value)
    diag = jnp.sum(jnp.where(lane == rows + 96, block[count], 0.0), axis=1, keepdims=True)
    scale = jnp.broadcast_to(jnp.sqrt(diag / total + 1e-06), (8, 128))

    def spread(value, column):
        return jnp.broadcast_to(value[:, column : column + 1], (8, 128))

    def row_of(parts, row):
        return jnp.broadcast_to(parts[row // 8][row % 8 : row % 8 + 1, :], (8, 128))

    for start in range(0, count, group):
        size = 8 * group
        first = 8 * start
        square = [
            [spread(block[start + p], first + m) * one for p in range(group)] for m in range(size)
        ]
        below = {
            i: [spread(block[i], first + m) for m in range(size)]
            for i in range(start + group, count + 1)
        }
        panel = []
        for p in range(group):
            unit = (lane == rows + first + 8 * p).astype(jnp.float32)
            inside = (lane >= first) & (lane < first + size)
            panel.append(jnp.where(inside, -unit, block[start + p]))
        inverses = []
        for m in range(size):
            inverses.append(1.0 / row_of(square[m], m))
            factor = [
                jnp.where(rows == m - 8 * p, 0.0, square[m][p]) if m // 8 == p else square[m][p]
                for p in range(group)
            ]
            for k in range(m + 1, size):
                line = row_of(square[k], m) * inverses[m]
                square[k] = [square[k][p] - factor[p] * line for p in range(group)]
            line = row_of(panel, m) * inverses[m]
            panel = [panel[p] - factor[p] * line for p in range(group)]
        lines = [row_of(panel, m) * inverses[m] for m in range(size)]
        for i in below:
            terms = [below[i][m] * lines[m] for m in range(size)]
            while len(terms) > 1:
                terms = [terms[t] + terms[t + 1] for t in range(0, len(terms), 2)]
            outside = (lane < first) | (lane >= first + size)
            block[i] = jnp.where(outside, block[i], 0.0) - terms[0]
    answer = jnp.where(lane < 96, block[count], 0.0)
    coef_ref[...] = answer[:6, :96]
    predicted = jnp.dot(answer, z_ref[...], precision=PRECISE, preferred_element_type=jnp.float32)
    residual = (z_ref[pl.ds(96, 8), :] - predicted) / scale
    picked = jnp.zeros((8, 128), jnp.float32)
    for place in range(4):
        even = pltpu.roll(residual, (128 - 16 * place) % 128, 1) if place else residual
        odd = pltpu.roll(residual, 112 - 16 * place, 1)
        picked = jnp.where(lane // 16 == place, jnp.where(core == 0, even, odd), picked)
    res_ref[...] = picked[:6, :64]


def crosswise(value, axis, target):
    pairs = []
    for chip in range(lax.axis_size(axis)):
        for core in range(2):
            pairs.append((2 * chip + core, 2 * target(chip) + 1 - core))
    return lax.ppermute(value, (axis, "gz"), pairs)


def moved(value, axis, step):
    size = lax.axis_size(axis)
    return crosswise(value, axis, lambda chip: (chip + step) % size)


def added_up(value, axis):
    bit = 1
    while bit < lax.axis_size(axis):
        value = value + crosswise(value, axis, lambda chip: chip ^ bit)
        bit *= 2
    return value


def call(kernel, outs, scratch, place=pltpu.VMEM):
    def run(*args):
        return pl.pallas_call(
            kernel,
            out_shape=[jax.ShapeDtypeStruct(shape, jnp.float32) for shape in outs],
            in_specs=[pl.BlockSpec(memory_space=place)] * len(args),
            out_specs=[pl.BlockSpec(memory_space=pltpu.VMEM)] * len(outs),
            scratch_shapes=scratch,
            compiler_params=pltpu.CompilerParams(vmem_limit_bytes=8 * 2**20),
        )(*args)

    return run


def chip_shards(velocity):
    bx, by, bz = velocity.shape[1:]
    chips = lax.axis_size("gy")
    length = bz * lax.axis_size("gz")
    low_type, wide_type = jnp.bfloat16, jnp.float32
    tables = [
        velocity_plane_table(bx, by),
        pair_plane_table(bx, by),
        line_table(length, ((3.0, False), (3.0, True), (6.0, False), (6.0, True))),
        line_table(length, ((12.0, False), (12.0, True), (6.0, False), (0.0, False))),
    ]
    tables = [jnp.asarray(table, low_type) for table in tables]
    shapes = [tables[0].shape, tables[1].shape, (bz, 128), (bz, 128)]
    (part,) = call(
        sums_kernel,
        [(ROWS + 3 * FACE, 128)],
        [pltpu.VMEM(velocity.shape, wide_type)]
        + [pltpu.VMEM(shape, low_type) for shape in shapes]
        + [pltpu.VMEM((8 * shapes[1][0], 128), wide_type), pltpu.SemaphoreType.DMA((7,))],
        pltpu.HBM,
    )(*[pltpu.with_memory_space_constraint(value, pltpu.HBM) for value in (velocity, *tables)])
    part = part + lax.ppermute(part, "gz", [(0, 1), (1, 0)])
    own = part[: ROWS + FACE]
    low = moved(part[ROWS + FACE : ROWS + 2 * FACE], "gx", -1)
    high = moved(part[ROWS + 2 * FACE :], "gx", 1)
    left = jnp.arange(128, dtype=jnp.int32)[None, :] < 64
    middle = jnp.zeros((ROWS - FACE, 128), wide_type)
    own = own + jnp.concatenate(
        [jnp.where(left, high, low), middle, jnp.where(left, low, high)], axis=0
    )

    near = jnp.stack([own, crosswise(own, "gy", lambda chip: chip ^ 1)])
    far = crosswise(near, "gy", lambda chip: chip ^ 2)
    stacked, gram = call(
        features_kernel,
        [(128, 128), (104, 128)],
        [
            pltpu.VMEM((chips, ROWS + FACE, 128), wide_type),
            pltpu.VMEM((27 * chips, 128), wide_type),
            pltpu.VMEM((chips, 128, 128), wide_type),
        ],
    )(near, far)
    gram = added_up(gram, "gx")
    samples = (bx // 8) * (by // 8) * (length // 8)
    total = float(samples * lax.axis_size("gx") * chips)
    residual, coefficients = call(
        functools.partial(solve_kernel, total), [(6, 64), (6, 96)], []
    )(gram, stacked)
    return (residual, coefficients.T)


def chip_form(mesh, velocity):
    shape = mesh.shape
    brick = (velocity.shape[1] // shape["gx"], velocity.shape[2] // shape["gy"])
    even = shape["gx"] & (shape["gx"] - 1) == 0
    return (
        even and shape["gy"] == 4 and shape["gz"] == 2
        and brick == (16, 16) and velocity.shape[3] == 256
    )


def solution(mesh):
    in_specs = (P(None, "gx", "gy", "gz"),)
    out_specs = (P(None, ("gx", "gy", "gz")), P())

    def run(velocity):
        body = chip_shards if chip_form(mesh, velocity) else shards
        return jax.shard_map(
            body, mesh=mesh, in_specs=in_specs, out_specs=out_specs, check_vma=False
        )(velocity)

    return run
```

```python
import functools

import jax
import jax.numpy as jnp
import numpy as np
from jax import lax
from jax.experimental import pallas as pl
from jax.experimental.pallas import tpu as pltpu
from jax.sharding import PartitionSpec as P

PRECISE = lax.Precision.HIGHEST
INDEX_PAIRS = ((0, 0), (1, 1), (2, 2), (0, 1), (0, 2), (1, 2))
WIDTHS = (3.0, 6.0, 12.0)


def extended(block, sides, width):
    for axis, dim in sides:
        count = lax.axis_size(axis)
        forward = [(i, i + 1) for i in range(count - 1)]
        forward.append((count - 1, 0))
        backward = [(target, source) for source, target in forward]
        low = lax.ppermute(
            lax.slice_in_dim(block, block.shape[dim] - width, None, axis=dim), axis, forward
        )
        high = lax.ppermute(lax.slice_in_dim(block, 0, width, axis=dim), axis, backward)
        block = jnp.concatenate([low, block, high], axis=dim)
    return block


def window_table(combos):
    weights_table = np.zeros((len(combos), 16), np.float32)
    for row_index in range(len(combos)):
        box_width, offset = combos[row_index]
        low_edge = 7.5 + offset - box_width / 2.0
        high_edge = 7.5 + offset + box_width / 2.0
        for cell_index in range(16):
            cell_share = min(cell_index + 0.5, high_edge) - max(cell_index - 0.5, low_edge)
            weights_table[row_index, cell_index] = max(cell_share, 0.0) / box_width
    return weights_table


def velocity_combos():
    return [(box_width, offset) for box_width in WIDTHS for offset in (-2.0, 0.0, 2.0)]


def product_combos():
    return [(3.0, 0.0), (12.0, 0.0)]


def matrix_product(left_matrix, right_matrix):
    return [
        [
            left_matrix[i][0] * right_matrix[0][j]
            + left_matrix[i][1] * right_matrix[1][j]
            + left_matrix[i][2] * right_matrix[2][j]
            for j in range(3)
        ]
        for i in range(3)
    ]


def pick_pairs(matrix):
    return [matrix[i][j] for i, j in INDEX_PAIRS]


def build_rows(box_means, pair_means):
    feature_rows = []
    centre_values = []
    for width_index in range(3):
        middle = 3 * width_index + 1
        scaled = WIDTHS[width_index] ** 2 * 0.25

        def offset_value(component, direction, step_size):
            position_list = [middle, middle, middle]
            position_list[direction] = middle + step_size
            return box_means[component, position_list[0], position_list[1], position_list[2]]

        centre_values.append([box_means[i, middle, middle, middle] for i in range(3)])
        gradient = [
            [(offset_value(i, j, 1) - offset_value(i, j, -1)) * scaled for j in range(3)]
            for i in range(3)
        ]
        strain = [[(gradient[i][j] + gradient[j][i]) * 0.5 for j in range(3)] for i in range(3)]
        spin_part = [[(gradient[i][j] - gradient[j][i]) * 0.5 for j in range(3)] for i in range(3)]
        square_strain = matrix_product(strain, strain)
        first_order = matrix_product(strain, spin_part)
        second_order = matrix_product(spin_part, strain)
        commutator = [[first_order[i][j] - second_order[i][j] for j in range(3)] for i in range(3)]
        spin_square = matrix_product(spin_part, spin_part)
        magnitude = sum((strain[i][j] * strain[i][j] for i in range(3) for j in range(3)))
        feature_rows += (
            pick_pairs(strain)
            + pick_pairs(square_strain)
            + pick_pairs(commutator)
            + pick_pairs(spin_square)
        )
        feature_rows += [magnitude * entry for entry in pick_pairs(strain)]
    small_box = centre_values[0]
    large_box = centre_values[2]
    feature_rows += [
        pair_means[index, 0] - small_box[i] * small_box[j]
        for index, (i, j) in enumerate(INDEX_PAIRS)
    ]
    target_rows = [
        pair_means[index, 1] - large_box[i] * large_box[j]
        for index, (i, j) in enumerate(INDEX_PAIRS)
    ]
    return (jnp.stack(feature_rows), jnp.stack(target_rows))


def solve_fit(gram_matrix, sample_total):
    scales = jnp.sqrt(jnp.diagonal(gram_matrix) / sample_total + 1e-06)
    feature_scale = scales[:96]
    normal = gram_matrix[:96, :96] / (
        sample_total * feature_scale[:, None] * feature_scale[None, :]
    ) + 0.1 * jnp.eye(96, dtype=jnp.float32)
    target_side = gram_matrix[:96, 96:] / (sample_total * feature_scale[:, None])
    factor = jnp.linalg.cholesky(normal)
    solved = jax.scipy.linalg.cho_solve((factor, True), target_side)
    return (solved / feature_scale[:, None], scales[96:])


def axis_weights(length, weights_table):
    sample_count = length // 8
    combo_count = weights_table.shape[0]
    full_table = np.zeros((sample_count * combo_count, length + 8), np.float32)
    for sample_index in range(sample_count):
        full_table[
            sample_index * combo_count : (sample_index + 1) * combo_count,
            8 * sample_index : 8 * sample_index + 16,
        ] = weights_table
    return jnp.asarray(full_table)


def windowed(wide_field, weights_table):
    along_z = jnp.einsum(
        "cxyz,kz->cxyk",
        wide_field,
        axis_weights(wide_field.shape[3] - 8, weights_table),
        precision=PRECISE,
    )
    along_y = jnp.einsum(
        "cxyk,jy->cxjk",
        along_z,
        axis_weights(wide_field.shape[2] - 8, weights_table),
        precision=PRECISE,
    )
    return jnp.einsum(
        "cxjk,ix->cijk",
        along_y,
        axis_weights(wide_field.shape[1] - 8, weights_table),
        precision=PRECISE,
    )


def shards(velocity):
    rounded = velocity.astype(jnp.bfloat16)
    padded = extended(rounded, (("gx", 1), ("gy", 2), ("gz", 3)), 4)
    wide_field = padded.astype(jnp.float32)
    count_x = velocity.shape[1] // 8
    count_y = velocity.shape[2] // 8
    count_z = velocity.shape[3] // 8
    samples = count_x * count_y * count_z
    box_means = windowed(wide_field, window_table(velocity_combos()))
    box_means = box_means.reshape(3, count_x, 9, count_y, 9, count_z, 9)
    box_means = jnp.transpose(box_means, (0, 2, 4, 6, 1, 3, 5)).reshape(3, 9, 9, 9, samples)
    pair_field = jnp.stack([wide_field[i] * wide_field[j] for i, j in INDEX_PAIRS])
    pair_means = windowed(pair_field, window_table(product_combos())).reshape(
        6, count_x, 2, count_y, 2, count_z, 2
    )
    pair_means = jnp.stack(
        [pair_means[:, :, 0, :, 0, :, 0], pair_means[:, :, 1, :, 1, :, 1]], axis=1
    )
    pair_means = pair_means.reshape(6, 2, samples)
    features, targets = build_rows(box_means, pair_means)
    stacked = jnp.concatenate([features, targets], axis=0)
    local_gram = jnp.dot(stacked, stacked.T, precision=PRECISE, preferred_element_type=jnp.float32)
    gram_matrix = lax.psum(local_gram, ("gx", "gy", "gz"))
    sample_total = float(samples * lax.axis_size("gx") * lax.axis_size("gy") * lax.axis_size("gz"))
    coefficients, target_scale = solve_fit(gram_matrix, sample_total)
    predicted = jnp.dot(
        coefficients.T, features, precision=PRECISE, preferred_element_type=jnp.float32
    )
    residual = (targets - predicted) / target_scale[:, None]
    return (residual, coefficients)


OWN = ((0, 0), (0, 1), (1, 0), (1, 1))
FACE_LOW = ((-1, -1), (-1, 2), (-1, 0), (-1, 1))
FACE_HIGH = ((2, 0), (2, 1), (2, -1), (2, 2))
FACE_Y = ((1, -1), (1, 2), (0, -1), (0, 2))
ROWS, FACE = 48, 24


def share(centre, width, cell):
    part = min(cell + 0.5, centre + width / 2) - max(cell - 0.5, centre - width / 2)
    return max(part, 0.0)


def window(length, width, sample, difference, turns=(0,)):
    total = np.zeros(length)
    for shift, sign in ((2.0, 1.0), (-2.0, -1.0)) if difference else ((0.0, 1.0),):
        for cell in range(length):
            for turn in turns:
                total[cell] += sign * share(
                    8 * sample + 3.5 + shift, width, cell + turn * length
                )
    return total


def plane_row(bx, by, place, width, direction):
    return np.outer(
        window(bx, width, place[0], direction == 0), window(by, width, place[1], direction == 1)
    ).reshape(-1)


def velocity_plane_table(bx, by):
    none = np.zeros(bx * by)
    rows = []
    for place in OWN:
        three = [plane_row(bx, by, place, 3.0, k) for k in (0, 1, 2)]
        six = [plane_row(bx, by, place, 6.0, k) for k in (0, 1, 2)]
        rows += three + [three[2]] + six + [none]
    for places in (OWN, FACE_LOW, FACE_HIGH, FACE_Y):
        for place in places:
            twelve = [plane_row(bx, by, place, 12.0, k) for k in (0, 1, 2)]
            along = {FACE_LOW: 0, FACE_HIGH: 0, FACE_Y: 1}.get(places)
            last = none if along is None else plane_row(bx, by, place, 6.0, along)
            rows += twelve + [twelve[2], last, none, none, none]
    return np.stack(rows)


def pair_plane_table(bx, by):
    rows = [plane_row(bx, by, place, 3.0, 2) for place in OWN]
    for places in (OWN, FACE_LOW, FACE_HIGH, FACE_Y):
        rows += [plane_row(bx, by, place, 12.0, 2) for place in places]
    while len(rows) % 16:
        rows.append(np.zeros(bx * by))
    return np.stack(rows)


def line_table(length, blocks):
    columns = []
    for width, difference in blocks:
        for sample in range(length // 8):
            if width:
                columns.append(window(length, width, sample, difference, (-1, 0, 1)))
            else:
                columns.append(np.zeros(length))
    return np.stack(columns, axis=1)


def three_parts(value):
    high = value.astype(jnp.bfloat16)
    rest = value - high.astype(jnp.float32)
    middle = rest.astype(jnp.bfloat16)
    low = (rest - middle.astype(jnp.float32)).astype(jnp.bfloat16)
    return high, middle, low


def mxu(left, right):
    return jnp.dot(left, right, preferred_element_type=jnp.float32)


def sums_kernel(x_hbm, wv_hbm, wp_hbm, la_hbm, lb_hbm, out_ref, x_ref, wv, wp, la, lb, pair_ref, sems):
    core = lax.axis_index("gz")
    cells = x_ref.shape[1] * x_ref.shape[2]
    length = x_ref.shape[3]
    begin = pl.multiple_of(core * length, length)
    copies = [pltpu.make_async_copy(wv_hbm, wv, sems.at[0])]
    copies += [pltpu.make_async_copy(x_hbm.at[c], x_ref.at[c], sems.at[1 + c]) for c in range(3)]
    copies += [pltpu.make_async_copy(wp_hbm, wp, sems.at[4])]
    copies += [pltpu.make_async_copy(la_hbm.at[pl.ds(begin, length)], la, sems.at[5])]
    copies += [pltpu.make_async_copy(lb_hbm.at[pl.ds(begin, length)], lb, sems.at[6])]
    for copy in copies:
        copy.start()
    rows = lax.broadcasted_iota(jnp.int32, (8, 128), 0)
    lanes = lax.broadcasted_iota(jnp.int32, (8, 128), 1) // 32
    pair_ref[...] = jnp.zeros(pair_ref.shape, jnp.float32)

    def gathered(groups, blocks):
        total = jnp.zeros((8, 128), jnp.float32)
        for place in range(4):
            base = merged = groups[8 * place : 8 * place + 8]
            for block, chosen in blocks:
                hit = rows == chosen[0]
                for row in chosen[1:]:
                    hit = hit | (rows == row)
                merged = jnp.where(hit, pltpu.roll(base, 128 - 32 * block, 1), merged)
            if place:
                merged = pltpu.roll(merged, 32 * place, 1)
            total = jnp.where(lanes == place, merged, total)
        return total

    for copy in copies:
        copy.wait()
    fields = [x_ref[c].reshape(cells, length).astype(jnp.bfloat16) for c in range(3)]
    planes = [mxu(wv[...], field) for field in fields]
    wide = [field.astype(jnp.float32) for field in fields]
    count = wp.shape[0]
    weights = jnp.concatenate([wp[...], wp[...]], axis=1)
    for pair, (i, j) in enumerate(INDEX_PAIRS):
        product = wide[i] * wide[j]
        high = product.astype(jnp.bfloat16)
        low = (product - high.astype(jnp.float32)).astype(jnp.bfloat16)
        pair_ref[pl.ds(pair, count, stride=8), :] = mxu(
            weights, jnp.concatenate([high, low], axis=0)
        )

    def along_line(value, line):
        high, middle, low = three_parts(value)
        return mxu(
            jnp.concatenate([high, middle], axis=1), jnp.concatenate([line, line], axis=0)
        ) + mxu(low, line)

    narrow = along_line(
        jnp.concatenate([plane[:32] for plane in planes] + [pair_ref[pl.ds(0, 32), :]], axis=0),
        la[...],
    )
    broad = along_line(
        jnp.concatenate([plane[32:] for plane in planes] + [pair_ref[pl.ds(32, 128), :]], axis=0),
        lb[...],
    )
    for c in range(3):
        value = gathered(narrow[32 * c : 32 * c + 32], ((1, (2,)), (2, (4, 5)), (3, (6,))))
        out_ref[pl.ds(27 + 3 * c, 3), :] = value[0:3]
        out_ref[pl.ds(36 + c, 1), :] = value[3:4]
        out_ref[pl.ds(12 + c, 1), :] = value[4:5]
        out_ref[pl.ds(21 + c, 1), :] = value[5:6]
        out_ref[pl.ds(24 + c, 1), :] = value[6:7]
        for part in range(4):
            at = 128 * c + 32 * part
            base = (0, ROWS + FACE, ROWS + 2 * FACE, ROWS)[part]
            blocks = ((1, (2,)), (2, (4,))) if part else ((1, (2,)),)
            value = gathered(broad[at : at + 32], blocks)
            out_ref[pl.ds(base + 3 * c, 3), :] = value[0:3]
            out_ref[pl.ds(base + 9 + c, 1), :] = value[3:4]
            if part:
                live, still = (12, 21) if part < 3 else (21, 12)
                out_ref[pl.ds(base + live + c, 1), :] = value[4:5]
                out_ref[pl.ds(base + still + c, 1), :] = jnp.zeros((1, 128), jnp.float32)
    out_ref[pl.ds(39, 6), :] = gathered(narrow[96:128], ())[:6]
    out_ref[pl.ds(45, 3), :] = jnp.zeros((3, 128), jnp.float32)
    for part in range(4):
        base = (0, ROWS + FACE, ROWS + 2 * FACE, ROWS)[part]
        out_ref[pl.ds(base + 15, 6), :] = gathered(broad[384 + 32 * part : 416 + 32 * part], ())[:6]


def features_kernel(near_ref, far_ref, z_out, gram_ref, b_ref, a_ref, z_ref):
    mine = lax.axis_index("gy")
    chips = b_ref.shape[0]
    for slot in range(chips):
        b_ref[jnp.bitwise_xor(mine, slot)] = near_ref[slot] if slot < 2 else far_ref[slot - 2]
    lane = lax.broadcasted_iota(jnp.int32, (FACE, 128), 1)
    upper = (lane // 32) % 2 == 1
    z_ref[:, 96:, :] = jnp.zeros((chips, 32, 128), jnp.float32)
    for chip in range(chips):
        after = pltpu.roll(b_ref[(chip + 1) % chips, ROWS:, :], 96, 1)
        before = pltpu.roll(b_ref[(chip - 1) % chips, ROWS:, :], 32, 1)
        sums = b_ref[chip, :FACE, :] + jnp.where(upper, after, before)
        base = 27 * chip
        a_ref[pl.ds(base, 9), :] = b_ref[chip, 27:36, :]
        a_ref[pl.ds(base + 9, 3, stride=3), :] = sums[12:15]
        a_ref[pl.ds(base + 10, 3, stride=3), :] = sums[21:24]
        a_ref[pl.ds(base + 11, 3, stride=3), :] = b_ref[chip, 24:27, :]
        a_ref[pl.ds(base + 18, 9), :] = sums[0:9]
        for at, centres, products, width in (
            (90, b_ref[chip, 36:39, :], b_ref[chip, 39:45, :], 3.0),
            (96, sums[9:12], sums[15:21], 12.0),
        ):
            means = [centres[c : c + 1] * (1.0 / width**3) for c in range(3)]
            for pair, (i, j) in enumerate(INDEX_PAIRS):
                z_ref[chip, pl.ds(at + pair, 1), :] = (
                    products[pair : pair + 1] * (1.0 / width**3) - means[i] * means[j]
                )
    total = 3 * chips
    width = lax.broadcasted_iota(jnp.int32, (total, 128), 0) % 3
    factor = jnp.where(width == 0, 1.0 / 12.0, jnp.where(width == 1, 1.0 / 24.0, 1.0 / 48.0))
    grad = [
        [a_ref[pl.ds(3 * i + j, total, stride=9), :] * factor for j in range(3)] for i in range(3)
    ]
    strain = [[None] * 3 for _ in range(3)]
    spin = [[None] * 3 for _ in range(3)]
    for i in range(3):
        for j in range(i, 3):
            strain[i][j] = strain[j][i] = (grad[i][j] + grad[j][i]) * 0.5
            if i != j:
                spin[i][j] = (grad[i][j] - grad[j][i]) * 0.5
                spin[j][i] = (grad[j][i] - grad[i][j]) * 0.5

    def entry(left, right, i, j):
        terms = [
            left[i][k] * right[k][j]
            for k in range(3)
            if left[i][k] is not None and right[k][j] is not None
        ]
        return sum(terms[1:], terms[0])

    squares = [strain[i][j] * strain[i][j] for i in range(3) for j in range(3)]
    magnitude = sum(squares[1:], squares[0])
    columns = [strain[i][j] for i, j in INDEX_PAIRS]
    columns += [entry(strain, strain, i, j) for i, j in INDEX_PAIRS]
    columns += [entry(strain, spin, i, j) - entry(spin, strain, i, j) for i, j in INDEX_PAIRS]
    columns += [entry(spin, spin, i, j) for i, j in INDEX_PAIRS]
    columns += [magnitude * strain[i][j] for i, j in INDEX_PAIRS]
    for index, column in enumerate(columns):
        for chip in range(chips):
            z_ref[chip, pl.ds(index, 3, stride=30), :] = column[3 * chip : 3 * chip + 3]
    z_out[...] = z_ref[mine]
    stacked = jnp.concatenate([z_ref[chip] for chip in range(chips)], axis=1)
    gram = lax.dot_general(
        stacked[:104],
        stacked,
        (((1,), (1,)), ((), ())),
        precision=PRECISE,
        preferred_element_type=jnp.float32,
    )
    rows = lax.broadcasted_iota(jnp.int32, (8, 128), 0)
    lane = lax.broadcasted_iota(jnp.int32, (8, 128), 1)
    gram_ref[pl.ds(0, 8), :] = gram[:8]
    for p in range(1, 7):
        lower = pltpu.roll(gram[48 + 8 * p : 56 + 8 * p], 72, 1)
        gram_ref[pl.ds(8 * p, 8), :] = jnp.where(
            lane >= rows + 8 * p, gram[8 * p : 8 * p + 8], lower
        )


def solve_kernel(total, gram_ref, z_ref, res_ref, coef_ref):
    core = lax.axis_index("gz")
    one = jnp.where(core >= 0, 1.0, 2.0)
    count, group = 12, 2
    rows = lax.broadcasted_iota(jnp.int32, (8, 128), 0)
    lane = lax.broadcasted_iota(jnp.int32, (8, 128), 1)
    half = []
    for i in range(count + 1):
        if i < 7:
            value = gram_ref[pl.ds(8 * i, 8), :]
            half.append(jnp.where(lane >= rows + 8 * i, value, 0.0))
        else:
            value = pltpu.roll(gram_ref[pl.ds(8 * i - 48, 8), :], 56, 1)
            half.append(jnp.where((lane >= 56) & (lane <= rows + 8 * i), value, 0.0))
    blank = [jnp.zeros((8, 128), jnp.float32)]
    other = jnp.transpose(jnp.concatenate(half + blank * (15 - count), axis=0))
    block = []
    for i in range(count + 1):
        value = half[i]
        ridge = value + 0.1 * (value + total * 1e-06) if i < count else value
        value = value + other[8 * i : 8 * i + 8]
        block.append(jnp.where(lane == rows + 8 * i, ridge, value))
    diag = jnp.sum(jnp.where(lane == rows + 96, block[count], 0.0), axis=1, keepdims=True)
    scale = jnp.broadcast_to(jnp.sqrt(diag / total + 1e-06), (8, 128))

    def spread(value, column):
        return jnp.broadcast_to(value[:, column : column + 1], (8, 128))

    def row_of(parts, row):
        return jnp.broadcast_to(parts[row // 8][row % 8 : row % 8 + 1, :], (8, 128))

    for start in range(0, count, group):
        size = 8 * group
        first = 8 * start
        near = range(start + group, min(start + 2 * group, count + 1))
        far = range(start + 2 * group, count + 1)
        square = [[spread(block[start + p], first + m) * one for p in range(group)] for m in range(size)]
        below = {i: [spread(block[i], first + m) for m in range(size)] for i in near}
        inside = (lane >= first) & (lane < first + size)
        panel = []
        for p in range(group):
            unit = (lane == rows + first + 8 * p).astype(jnp.float32)
            panel.append(jnp.where(inside, -unit, block[start + p]))
        inverses = []
        for m in range(size):
            inverses.append(1.0 / row_of(square[m], m))
            factor = [
                jnp.where(rows == m - 8 * p, 0.0, square[m][p]) if m // 8 == p else square[m][p]
                for p in range(group)
            ]
            for k in range(m + 1, size):
                line = row_of(square[k], m) * inverses[m]
                square[k] = [square[k][p] - factor[p] * line for p in range(group)]
            line = row_of(panel, m) * inverses[m]
            panel = [panel[p] - factor[p] * line for p in range(group)]
        lines = [row_of(panel, m) * inverses[m] for m in range(size)]
        for i in near:
            terms = [below[i][m] * lines[m] for m in range(size)]
            while len(terms) > 1:
                terms = [terms[t] + terms[t + 1] for t in range(0, len(terms), 2)]
            block[i] = jnp.where(inside, 0.0, block[i]) - terms[0]
        if far:
            scaled = []
            for p in range(group):
                inverse = inverses[8 * p]
                for row in range(1, 8):
                    inverse = jnp.where(rows == row, inverses[8 * p + row], inverse)
                scaled.append(panel[p] * inverse)
            blank = [jnp.zeros((8, 128), jnp.float32)]
            right = jnp.concatenate(blank * start + scaled + blank * (16 - group - start), axis=0)
            left = jnp.concatenate([jnp.where(inside, block[i], 0.0) for i in far], axis=0)
            change = jnp.dot(left, right, precision=PRECISE, preferred_element_type=jnp.float32)
            for at, i in enumerate(far):
                block[i] = jnp.where(inside, 0.0, block[i]) - change[8 * at : 8 * at + 8]
    answer = jnp.where(lane < 96, block[count], 0.0)
    coef_ref[...] = answer[:6, :96]
    predicted = jnp.dot(answer, z_ref[...], precision=PRECISE, preferred_element_type=jnp.float32)
    residual = (z_ref[pl.ds(96, 8), :] - predicted) / scale
    picked = jnp.zeros((8, 128), jnp.float32)
    for place in range(4):
        even = pltpu.roll(residual, (128 - 16 * place) % 128, 1) if place else residual
        odd = pltpu.roll(residual, 112 - 16 * place, 1)
        picked = jnp.where(lane // 16 == place, jnp.where(core == 0, even, odd), picked)
    res_ref[...] = picked[:6, :64]


def crosswise(value, axis, target):
    pairs = []
    for chip in range(lax.axis_size(axis)):
        for core in range(2):
            pairs.append((2 * chip + core, 2 * target(chip) + 1 - core))
    return lax.ppermute(value, (axis, "gz"), pairs)


def moved(value, axis, step):
    size = lax.axis_size(axis)
    return crosswise(value, axis, lambda chip: (chip + step) % size)


def added_up(value, axis):
    bit = 1
    while bit < lax.axis_size(axis):
        value = value + crosswise(value, axis, lambda chip: chip ^ bit)
        bit *= 2
    return value


def call(kernel, outs, scratch, place=pltpu.VMEM):
    def run(*args):
        return pl.pallas_call(
            kernel,
            out_shape=[jax.ShapeDtypeStruct(shape, jnp.float32) for shape in outs],
            in_specs=[pl.BlockSpec(memory_space=place)] * len(args),
            out_specs=[pl.BlockSpec(memory_space=pltpu.VMEM)] * len(outs),
            scratch_shapes=scratch,
            compiler_params=pltpu.CompilerParams(vmem_limit_bytes=8 * 2**20),
        )(*args)

    return run


def chip_shards(velocity):
    bx, by, bz = velocity.shape[1:]
    chips = lax.axis_size("gy")
    length = bz * lax.axis_size("gz")
    low_type, wide_type = jnp.bfloat16, jnp.float32
    tables = [
        velocity_plane_table(bx, by),
        pair_plane_table(bx, by),
        line_table(length, ((3.0, False), (3.0, True), (6.0, False), (6.0, True))),
        line_table(length, ((12.0, False), (12.0, True), (6.0, False), (0.0, False))),
    ]
    tables = [jnp.asarray(table, low_type) for table in tables]
    shapes = [tables[0].shape, tables[1].shape, (bz, 128), (bz, 128)]
    (part,) = call(
        sums_kernel,
        [(ROWS + 3 * FACE, 128)],
        [pltpu.VMEM(velocity.shape, wide_type)]
        + [pltpu.VMEM(shape, low_type) for shape in shapes]
        + [pltpu.VMEM((8 * shapes[1][0], 128), wide_type), pltpu.SemaphoreType.DMA((7,))],
        pltpu.HBM,
    )(*[pltpu.with_memory_space_constraint(value, pltpu.HBM) for value in (velocity, *tables)])
    part = part + lax.ppermute(part, "gz", [(0, 1), (1, 0)])
    own = part[: ROWS + FACE]
    low = moved(part[ROWS + FACE : ROWS + 2 * FACE], "gx", -1)
    high = moved(part[ROWS + 2 * FACE :], "gx", 1)
    left = jnp.arange(128, dtype=jnp.int32)[None, :] < 64
    middle = jnp.zeros((ROWS - FACE, 128), wide_type)
    own = own + jnp.concatenate(
        [jnp.where(left, high, low), middle, jnp.where(left, low, high)], axis=0
    )

    near = jnp.stack([own, crosswise(own, "gy", lambda chip: chip ^ 1)])
    far = crosswise(near, "gy", lambda chip: chip ^ 2)
    stacked, gram = call(
        features_kernel,
        [(128, 128), (56, 128)],
        [
            pltpu.VMEM((chips, ROWS + FACE, 128), wide_type),
            pltpu.VMEM((27 * chips, 128), wide_type),
            pltpu.VMEM((chips, 128, 128), wide_type),
        ],
    )(near, far)
    gram = added_up(gram, "gx")
    samples = (bx // 8) * (by // 8) * (length // 8)
    total = float(samples * lax.axis_size("gx") * chips)
    residual, coefficients = call(
        functools.partial(solve_kernel, total), [(6, 64), (6, 96)], []
    )(gram, stacked)
    return (residual, coefficients.T)


def chip_form(mesh, velocity):
    shape = mesh.shape
    brick = (velocity.shape[1] // shape["gx"], velocity.shape[2] // shape["gy"])
    even = shape["gx"] & (shape["gx"] - 1) == 0
    return (
        even and shape["gy"] == 4 and shape["gz"] == 2
        and brick == (16, 16) and velocity.shape[3] == 256
    )


def solution(mesh):
    in_specs = (P(None, "gx", "gy", "gz"),)
    out_specs = (P(None, ("gx", "gy", "gz")), P())

    def run(velocity):
        body = chip_shards if chip_form(mesh, velocity) else shards
        return jax.shard_map(
            body, mesh=mesh, in_specs=in_specs, out_specs=out_specs, check_vma=False
        )(velocity)

    return run
```

```python
import functools

import jax
import jax.numpy as jnp
import numpy as np
from jax import lax
from jax.experimental import pallas as pl
from jax.experimental.pallas import tpu as pltpu
from jax.sharding import PartitionSpec as P

PRECISE = lax.Precision.HIGHEST
INDEX_PAIRS = ((0, 0), (1, 1), (2, 2), (0, 1), (0, 2), (1, 2))
WIDTHS = (3.0, 6.0, 12.0)


def extended(block, sides, width):
    for axis, dim in sides:
        count = lax.axis_size(axis)
        forward = [(i, i + 1) for i in range(count - 1)]
        forward.append((count - 1, 0))
        backward = [(target, source) for source, target in forward]
        low = lax.ppermute(
            lax.slice_in_dim(block, block.shape[dim] - width, None, axis=dim), axis, forward
        )
        high = lax.ppermute(lax.slice_in_dim(block, 0, width, axis=dim), axis, backward)
        block = jnp.concatenate([low, block, high], axis=dim)
    return block


def window_table(combos):
    weights_table = np.zeros((len(combos), 16), np.float32)
    for row_index in range(len(combos)):
        box_width, offset = combos[row_index]
        low_edge = 7.5 + offset - box_width / 2.0
        high_edge = 7.5 + offset + box_width / 2.0
        for cell_index in range(16):
            cell_share = min(cell_index + 0.5, high_edge) - max(cell_index - 0.5, low_edge)
            weights_table[row_index, cell_index] = max(cell_share, 0.0) / box_width
    return weights_table


def velocity_combos():
    return [(box_width, offset) for box_width in WIDTHS for offset in (-2.0, 0.0, 2.0)]


def product_combos():
    return [(3.0, 0.0), (12.0, 0.0)]


def matrix_product(left_matrix, right_matrix):
    return [
        [
            left_matrix[i][0] * right_matrix[0][j]
            + left_matrix[i][1] * right_matrix[1][j]
            + left_matrix[i][2] * right_matrix[2][j]
            for j in range(3)
        ]
        for i in range(3)
    ]


def pick_pairs(matrix):
    return [matrix[i][j] for i, j in INDEX_PAIRS]


def build_rows(box_means, pair_means):
    feature_rows = []
    centre_values = []
    for width_index in range(3):
        middle = 3 * width_index + 1
        scaled = WIDTHS[width_index] ** 2 * 0.25

        def offset_value(component, direction, step_size):
            position_list = [middle, middle, middle]
            position_list[direction] = middle + step_size
            return box_means[component, position_list[0], position_list[1], position_list[2]]

        centre_values.append([box_means[i, middle, middle, middle] for i in range(3)])
        gradient = [
            [(offset_value(i, j, 1) - offset_value(i, j, -1)) * scaled for j in range(3)]
            for i in range(3)
        ]
        strain = [[(gradient[i][j] + gradient[j][i]) * 0.5 for j in range(3)] for i in range(3)]
        spin_part = [[(gradient[i][j] - gradient[j][i]) * 0.5 for j in range(3)] for i in range(3)]
        square_strain = matrix_product(strain, strain)
        first_order = matrix_product(strain, spin_part)
        second_order = matrix_product(spin_part, strain)
        commutator = [[first_order[i][j] - second_order[i][j] for j in range(3)] for i in range(3)]
        spin_square = matrix_product(spin_part, spin_part)
        magnitude = sum((strain[i][j] * strain[i][j] for i in range(3) for j in range(3)))
        feature_rows += (
            pick_pairs(strain)
            + pick_pairs(square_strain)
            + pick_pairs(commutator)
            + pick_pairs(spin_square)
        )
        feature_rows += [magnitude * entry for entry in pick_pairs(strain)]
    small_box = centre_values[0]
    large_box = centre_values[2]
    feature_rows += [
        pair_means[index, 0] - small_box[i] * small_box[j]
        for index, (i, j) in enumerate(INDEX_PAIRS)
    ]
    target_rows = [
        pair_means[index, 1] - large_box[i] * large_box[j]
        for index, (i, j) in enumerate(INDEX_PAIRS)
    ]
    return (jnp.stack(feature_rows), jnp.stack(target_rows))


def solve_fit(gram_matrix, sample_total):
    scales = jnp.sqrt(jnp.diagonal(gram_matrix) / sample_total + 1e-06)
    feature_scale = scales[:96]
    normal = gram_matrix[:96, :96] / (
        sample_total * feature_scale[:, None] * feature_scale[None, :]
    ) + 0.1 * jnp.eye(96, dtype=jnp.float32)
    target_side = gram_matrix[:96, 96:] / (sample_total * feature_scale[:, None])
    factor = jnp.linalg.cholesky(normal)
    solved = jax.scipy.linalg.cho_solve((factor, True), target_side)
    return (solved / feature_scale[:, None], scales[96:])


def axis_weights(length, weights_table):
    sample_count = length // 8
    combo_count = weights_table.shape[0]
    full_table = np.zeros((sample_count * combo_count, length + 8), np.float32)
    for sample_index in range(sample_count):
        full_table[
            sample_index * combo_count : (sample_index + 1) * combo_count,
            8 * sample_index : 8 * sample_index + 16,
        ] = weights_table
    return jnp.asarray(full_table)


def windowed(wide_field, weights_table):
    along_z = jnp.einsum(
        "cxyz,kz->cxyk",
        wide_field,
        axis_weights(wide_field.shape[3] - 8, weights_table),
        precision=PRECISE,
    )
    along_y = jnp.einsum(
        "cxyk,jy->cxjk",
        along_z,
        axis_weights(wide_field.shape[2] - 8, weights_table),
        precision=PRECISE,
    )
    return jnp.einsum(
        "cxjk,ix->cijk",
        along_y,
        axis_weights(wide_field.shape[1] - 8, weights_table),
        precision=PRECISE,
    )


def shards(velocity):
    rounded = velocity.astype(jnp.bfloat16)
    padded = extended(rounded, (("gx", 1), ("gy", 2), ("gz", 3)), 4)
    wide_field = padded.astype(jnp.float32)
    count_x = velocity.shape[1] // 8
    count_y = velocity.shape[2] // 8
    count_z = velocity.shape[3] // 8
    samples = count_x * count_y * count_z
    box_means = windowed(wide_field, window_table(velocity_combos()))
    box_means = box_means.reshape(3, count_x, 9, count_y, 9, count_z, 9)
    box_means = jnp.transpose(box_means, (0, 2, 4, 6, 1, 3, 5)).reshape(3, 9, 9, 9, samples)
    pair_field = jnp.stack([wide_field[i] * wide_field[j] for i, j in INDEX_PAIRS])
    pair_means = windowed(pair_field, window_table(product_combos())).reshape(
        6, count_x, 2, count_y, 2, count_z, 2
    )
    pair_means = jnp.stack(
        [pair_means[:, :, 0, :, 0, :, 0], pair_means[:, :, 1, :, 1, :, 1]], axis=1
    )
    pair_means = pair_means.reshape(6, 2, samples)
    features, targets = build_rows(box_means, pair_means)
    stacked = jnp.concatenate([features, targets], axis=0)
    local_gram = jnp.dot(stacked, stacked.T, precision=PRECISE, preferred_element_type=jnp.float32)
    gram_matrix = lax.psum(local_gram, ("gx", "gy", "gz"))
    sample_total = float(samples * lax.axis_size("gx") * lax.axis_size("gy") * lax.axis_size("gz"))
    coefficients, target_scale = solve_fit(gram_matrix, sample_total)
    predicted = jnp.dot(
        coefficients.T, features, precision=PRECISE, preferred_element_type=jnp.float32
    )
    residual = (targets - predicted) / target_scale[:, None]
    return (residual, coefficients)


OWN = ((0, 0), (0, 1), (1, 0), (1, 1))
FACE_LOW = ((-1, -1), (-1, 2), (-1, 0), (-1, 1))
FACE_HIGH = ((2, 0), (2, 1), (2, -1), (2, 2))
FACE_Y = ((1, -1), (1, 2), (0, -1), (0, 2))
ROWS, FACE = 48, 24


def share(centre, width, cell):
    part = min(cell + 0.5, centre + width / 2) - max(cell - 0.5, centre - width / 2)
    return max(part, 0.0)


def window(length, width, sample, difference, turns=(0,)):
    total = np.zeros(length)
    for shift, sign in ((2.0, 1.0), (-2.0, -1.0)) if difference else ((0.0, 1.0),):
        for cell in range(length):
            for turn in turns:
                total[cell] += sign * share(
                    8 * sample + 3.5 + shift, width, cell + turn * length
                )
    return total


def plane_row(bx, by, place, width, direction):
    return np.outer(
        window(bx, width, place[0], direction == 0), window(by, width, place[1], direction == 1)
    ).reshape(-1)


def velocity_plane_table(bx, by):
    none = np.zeros(bx * by)
    rows = []
    for place in OWN:
        three = [plane_row(bx, by, place, 3.0, k) for k in (0, 1, 2)]
        six = [plane_row(bx, by, place, 6.0, k) for k in (0, 1, 2)]
        rows += three + [three[2]] + six + [none]
    for places in (OWN, FACE_LOW, FACE_HIGH, FACE_Y):
        for place in places:
            twelve = [plane_row(bx, by, place, 12.0, k) for k in (0, 1, 2)]
            along = {FACE_LOW: 0, FACE_HIGH: 0, FACE_Y: 1}.get(places)
            last = none if along is None else plane_row(bx, by, place, 6.0, along)
            rows += twelve + [twelve[2], last, none, none, none]
    return np.stack(rows)


def pair_plane_table(bx, by):
    rows = [plane_row(bx, by, place, 3.0, 2) for place in OWN]
    for places in (OWN, FACE_LOW, FACE_HIGH, FACE_Y):
        rows += [plane_row(bx, by, place, 12.0, 2) for place in places]
    while len(rows) % 16:
        rows.append(np.zeros(bx * by))
    return np.stack(rows)


def line_table(length, blocks):
    columns = []
    for width, difference in blocks:
        for sample in range(length // 8):
            if width:
                columns.append(window(length, width, sample, difference, (-1, 0, 1)))
            else:
                columns.append(np.zeros(length))
    return np.stack(columns, axis=1)


def three_parts(value):
    high = value.astype(jnp.bfloat16)
    rest = value - high.astype(jnp.float32)
    middle = rest.astype(jnp.bfloat16)
    low = (rest - middle.astype(jnp.float32)).astype(jnp.bfloat16)
    return high, middle, low


def mxu(left, right):
    return jnp.dot(left, right, preferred_element_type=jnp.float32)


def sums_kernel(x_hbm, wv_hbm, wp_hbm, la_hbm, lb_hbm, out_ref, x_ref, wv, wp, la, lb, pair_ref, sems):
    core = lax.axis_index("gz")
    cells = x_ref.shape[1] * x_ref.shape[2]
    length = x_ref.shape[3]
    begin = pl.multiple_of(core * length, length)
    copies = [pltpu.make_async_copy(wv_hbm, wv, sems.at[0])]
    copies += [pltpu.make_async_copy(x_hbm.at[c], x_ref.at[c], sems.at[1 + c]) for c in range(3)]
    copies += [pltpu.make_async_copy(wp_hbm, wp, sems.at[4])]
    copies += [pltpu.make_async_copy(la_hbm.at[pl.ds(begin, length)], la, sems.at[5])]
    copies += [pltpu.make_async_copy(lb_hbm.at[pl.ds(begin, length)], lb, sems.at[6])]
    for copy in copies:
        copy.start()
    rows = lax.broadcasted_iota(jnp.int32, (8, 128), 0)
    lanes = lax.broadcasted_iota(jnp.int32, (8, 128), 1) // 32
    pair_ref[...] = jnp.zeros(pair_ref.shape, jnp.float32)

    def gathered(groups, blocks):
        total = jnp.zeros((8, 128), jnp.float32)
        for place in range(4):
            base = merged = groups[8 * place : 8 * place + 8]
            for block, chosen in blocks:
                hit = rows == chosen[0]
                for row in chosen[1:]:
                    hit = hit | (rows == row)
                merged = jnp.where(hit, pltpu.roll(base, 128 - 32 * block, 1), merged)
            if place:
                merged = pltpu.roll(merged, 32 * place, 1)
            total = jnp.where(lanes == place, merged, total)
        return total

    for copy in copies:
        copy.wait()
    fields = [x_ref[c].reshape(cells, length).astype(jnp.bfloat16) for c in range(3)]
    planes = [mxu(wv[...], field) for field in fields]
    wide = [field.astype(jnp.float32) for field in fields]
    count = wp.shape[0]
    weights = jnp.concatenate([wp[...], wp[...]], axis=1)
    for pair, (i, j) in enumerate(INDEX_PAIRS):
        product = wide[i] * wide[j]
        high = product.astype(jnp.bfloat16)
        low = (product - high.astype(jnp.float32)).astype(jnp.bfloat16)
        pair_ref[pl.ds(pair, count, stride=8), :] = mxu(
            weights, jnp.concatenate([high, low], axis=0)
        )

    def along_line(value, line):
        high, middle, low = three_parts(value)
        return mxu(
            jnp.concatenate([high, middle], axis=1), jnp.concatenate([line, line], axis=0)
        ) + mxu(low, line)

    narrow = along_line(
        jnp.concatenate([plane[:32] for plane in planes] + [pair_ref[pl.ds(0, 32), :]], axis=0),
        la[...],
    )
    broad = along_line(
        jnp.concatenate([plane[32:] for plane in planes] + [pair_ref[pl.ds(32, 128), :]], axis=0),
        lb[...],
    )
    for c in range(3):
        value = gathered(narrow[32 * c : 32 * c + 32], ((1, (2,)), (2, (4, 5)), (3, (6,))))
        out_ref[pl.ds(27 + 3 * c, 3), :] = value[0:3]
        out_ref[pl.ds(36 + c, 1), :] = value[3:4]
        out_ref[pl.ds(12 + c, 1), :] = value[4:5]
        out_ref[pl.ds(21 + c, 1), :] = value[5:6]
        out_ref[pl.ds(24 + c, 1), :] = value[6:7]
        for part in range(4):
            at = 128 * c + 32 * part
            base = (0, ROWS + FACE, ROWS + 2 * FACE, ROWS)[part]
            blocks = ((1, (2,)), (2, (4,))) if part else ((1, (2,)),)
            value = gathered(broad[at : at + 32], blocks)
            out_ref[pl.ds(base + 3 * c, 3), :] = value[0:3]
            out_ref[pl.ds(base + 9 + c, 1), :] = value[3:4]
            if part:
                live, still = (12, 21) if part < 3 else (21, 12)
                out_ref[pl.ds(base + live + c, 1), :] = value[4:5]
                out_ref[pl.ds(base + still + c, 1), :] = jnp.zeros((1, 128), jnp.float32)
    out_ref[pl.ds(39, 6), :] = gathered(narrow[96:128], ())[:6]
    out_ref[pl.ds(45, 3), :] = jnp.zeros((3, 128), jnp.float32)
    for part in range(4):
        base = (0, ROWS + FACE, ROWS + 2 * FACE, ROWS)[part]
        out_ref[pl.ds(base + 15, 6), :] = gathered(broad[384 + 32 * part : 416 + 32 * part], ())[:6]


def features_kernel(own_ref, one_ref, swap_ref, both_ref, z_out, gram_ref, b_ref, a_ref, z_ref):
    mine = lax.axis_index("gy")
    chips = b_ref.shape[0]
    in_order(b_ref, mine, (own_ref, one_ref, swap_ref, both_ref))
    lane = lax.broadcasted_iota(jnp.int32, (FACE, 128), 1)
    upper = (lane // 32) % 2 == 1
    z_ref[:, 96:, :] = jnp.zeros((chips, 32, 128), jnp.float32)
    for chip in range(chips):
        after = pltpu.roll(b_ref[(chip + 1) % chips, ROWS:, :], 96, 1)
        before = pltpu.roll(b_ref[(chip - 1) % chips, ROWS:, :], 32, 1)
        sums = b_ref[chip, :FACE, :] + jnp.where(upper, after, before)
        base = 27 * chip
        a_ref[pl.ds(base, 9), :] = b_ref[chip, 27:36, :]
        a_ref[pl.ds(base + 9, 3, stride=3), :] = sums[12:15]
        a_ref[pl.ds(base + 10, 3, stride=3), :] = sums[21:24]
        a_ref[pl.ds(base + 11, 3, stride=3), :] = b_ref[chip, 24:27, :]
        a_ref[pl.ds(base + 18, 9), :] = sums[0:9]
        for at, centres, products, width in (
            (90, b_ref[chip, 36:39, :], b_ref[chip, 39:45, :], 3.0),
            (96, sums[9:12], sums[15:21], 12.0),
        ):
            means = [centres[c : c + 1] * (1.0 / width**3) for c in range(3)]
            for pair, (i, j) in enumerate(INDEX_PAIRS):
                z_ref[chip, pl.ds(at + pair, 1), :] = (
                    products[pair : pair + 1] * (1.0 / width**3) - means[i] * means[j]
                )
    total = 3 * chips
    width = lax.broadcasted_iota(jnp.int32, (total, 128), 0) % 3
    factor = jnp.where(width == 0, 1.0 / 12.0, jnp.where(width == 1, 1.0 / 24.0, 1.0 / 48.0))
    grad = [
        [a_ref[pl.ds(3 * i + j, total, stride=9), :] * factor for j in range(3)] for i in range(3)
    ]
    strain = [[None] * 3 for _ in range(3)]
    spin = [[None] * 3 for _ in range(3)]
    for i in range(3):
        for j in range(i, 3):
            strain[i][j] = strain[j][i] = (grad[i][j] + grad[j][i]) * 0.5
            if i != j:
                spin[i][j] = (grad[i][j] - grad[j][i]) * 0.5
                spin[j][i] = (grad[j][i] - grad[i][j]) * 0.5

    def entry(left, right, i, j):
        terms = [
            left[i][k] * right[k][j]
            for k in range(3)
            if left[i][k] is not None and right[k][j] is not None
        ]
        return sum(terms[1:], terms[0])

    squares = [strain[i][j] * strain[i][j] for i in range(3) for j in range(3)]
    magnitude = sum(squares[1:], squares[0])
    columns = [strain[i][j] for i, j in INDEX_PAIRS]
    columns += [entry(strain, strain, i, j) for i, j in INDEX_PAIRS]
    columns += [entry(strain, spin, i, j) - entry(spin, strain, i, j) for i, j in INDEX_PAIRS]
    columns += [entry(spin, spin, i, j) for i, j in INDEX_PAIRS]
    columns += [magnitude * strain[i][j] for i, j in INDEX_PAIRS]
    for index, column in enumerate(columns):
        for chip in range(chips):
            z_ref[chip, pl.ds(index, 3, stride=30), :] = column[3 * chip : 3 * chip + 3]
    z_out[...] = z_ref[mine]
    stacked = jnp.concatenate([z_ref[chip] for chip in range(chips)], axis=1)
    gram = lax.dot_general(
        stacked[:104],
        stacked,
        (((1,), (1,)), ((), ())),
        precision=PRECISE,
        preferred_element_type=jnp.float32,
    )
    rows = lax.broadcasted_iota(jnp.int32, (8, 128), 0)
    lane = lax.broadcasted_iota(jnp.int32, (8, 128), 1)
    gram_ref[pl.ds(0, 8), :] = gram[:8]
    for p in range(1, 7):
        lower = pltpu.roll(gram[48 + 8 * p : 56 + 8 * p], 72, 1)
        gram_ref[pl.ds(8 * p, 8), :] = jnp.where(
            lane >= rows + 8 * p, gram[8 * p : 8 * p + 8], lower
        )


def solve_kernel(total, own_ref, one_ref, swap_ref, both_ref, z_ref, res_ref, coef_ref, g_ref):
    core = lax.axis_index("gz")
    in_order(g_ref, lax.axis_index("gx"), (own_ref, one_ref, swap_ref, both_ref))
    packed = [
        (g_ref[0, pl.ds(8 * i, 8), :] + g_ref[1, pl.ds(8 * i, 8), :])
        + (g_ref[2, pl.ds(8 * i, 8), :] + g_ref[3, pl.ds(8 * i, 8), :])
        for i in range(7)
    ]
    one = jnp.where(core >= 0, 1.0, 2.0)
    count, group = 12, 2
    rows = lax.broadcasted_iota(jnp.int32, (8, 128), 0)
    lane = lax.broadcasted_iota(jnp.int32, (8, 128), 1)
    half = []
    for i in range(count + 1):
        if i < 7:
            value = packed[i]
            half.append(jnp.where(lane >= rows + 8 * i, value, 0.0))
        else:
            value = pltpu.roll(packed[i - 6], 56, 1)
            half.append(jnp.where((lane >= 56) & (lane <= rows + 8 * i), value, 0.0))
    blank = [jnp.zeros((8, 128), jnp.float32)]
    other = jnp.transpose(jnp.concatenate(half + blank * (15 - count), axis=0))
    block = []
    for i in range(count + 1):
        value = half[i]
        ridge = value + 0.1 * (value + total * 1e-06) if i < count else value
        value = value + other[8 * i : 8 * i + 8]
        block.append(jnp.where(lane == rows + 8 * i, ridge, value))
    diag = jnp.sum(jnp.where(lane == rows + 96, block[count], 0.0), axis=1, keepdims=True)
    scale = jnp.broadcast_to(jnp.sqrt(diag / total + 1e-06), (8, 128))

    def spread(value, column):
        return jnp.broadcast_to(value[:, column : column + 1], (8, 128))

    def row_of(parts, row):
        return jnp.broadcast_to(parts[row // 8][row % 8 : row % 8 + 1, :], (8, 128))

    for start in range(0, count, group):
        size = 8 * group
        first = 8 * start
        near = range(start + group, min(start + 2 * group, count + 1))
        far = range(start + 2 * group, count + 1)
        square = [[spread(block[start + p], first + m) * one for p in range(group)] for m in range(size)]
        below = {i: [spread(block[i], first + m) for m in range(size)] for i in near}
        inside = (lane >= first) & (lane < first + size)
        panel = []
        for p in range(group):
            unit = (lane == rows + first + 8 * p).astype(jnp.float32)
            panel.append(jnp.where(inside, -unit, block[start + p]))
        inverses = []
        for m in range(size):
            inverses.append(1.0 / row_of(square[m], m))
            factor = [
                jnp.where(rows == m - 8 * p, 0.0, square[m][p]) if m // 8 == p else square[m][p]
                for p in range(group)
            ]
            for k in range(m + 1, size):
                line = row_of(square[k], m) * inverses[m]
                square[k] = [square[k][p] - factor[p] * line for p in range(group)]
            line = row_of(panel, m) * inverses[m]
            panel = [panel[p] - factor[p] * line for p in range(group)]
        lines = [row_of(panel, m) * inverses[m] for m in range(size)]
        for i in near:
            terms = [below[i][m] * lines[m] for m in range(size)]
            while len(terms) > 1:
                terms = [terms[t] + terms[t + 1] for t in range(0, len(terms), 2)]
            block[i] = jnp.where(inside, 0.0, block[i]) - terms[0]
        if far:
            scaled = []
            for p in range(group):
                inverse = inverses[8 * p]
                for row in range(1, 8):
                    inverse = jnp.where(rows == row, inverses[8 * p + row], inverse)
                scaled.append(panel[p] * inverse)
            blank = [jnp.zeros((8, 128), jnp.float32)]
            right = jnp.concatenate(blank * start + scaled + blank * (16 - group - start), axis=0)
            left = jnp.concatenate([jnp.where(inside, block[i], 0.0) for i in far], axis=0)
            change = jnp.dot(left, right, precision=PRECISE, preferred_element_type=jnp.float32)
            for at, i in enumerate(far):
                block[i] = jnp.where(inside, 0.0, block[i]) - change[8 * at : 8 * at + 8]
    answer = jnp.where(lane < 96, block[count], 0.0)
    coef_ref[...] = answer[:6, :96]
    predicted = jnp.dot(answer, z_ref[...], precision=PRECISE, preferred_element_type=jnp.float32)
    residual = (z_ref[pl.ds(96, 8), :] - predicted) / scale
    picked = jnp.zeros((8, 128), jnp.float32)
    for place in range(4):
        even = pltpu.roll(residual, (128 - 16 * place) % 128, 1) if place else residual
        odd = pltpu.roll(residual, 112 - 16 * place, 1)
        picked = jnp.where(lane // 16 == place, jnp.where(core == 0, even, odd), picked)
    res_ref[...] = picked[:6, :64]


def crosswise(value, axis, target):
    pairs = []
    for chip in range(lax.axis_size(axis)):
        for core in range(2):
            pairs.append((2 * chip + core, 2 * target(chip) + 1 - core))
    return lax.ppermute(value, (axis, "gz"), pairs)


def moved(value, axis, step):
    size = lax.axis_size(axis)
    return crosswise(value, axis, lambda chip: (chip + step) % size)


def gathered_over(value, axis):
    pairs = []
    for chip in range(lax.axis_size(axis)):
        pairs += [(2 * chip, 2 * (chip ^ 1) + 1), (2 * chip + 1, 2 * (chip ^ 2))]
    both = crosswise(value, axis, lambda chip: chip ^ 3)
    one = lax.ppermute(value, (axis, "gz"), pairs)
    return value, one, lax.ppermute(one, "gz", [(0, 1), (1, 0)]), both


def in_order(target_ref, mine, refs):
    core = lax.axis_index("gz")
    own_ref, one_ref, swap_ref, both_ref = refs
    target_ref[mine] = own_ref[...]
    target_ref[jnp.bitwise_xor(mine, 2 - core)] = one_ref[...]
    target_ref[jnp.bitwise_xor(mine, 1 + core)] = swap_ref[...]
    target_ref[jnp.bitwise_xor(mine, 3)] = both_ref[...]


def call(kernel, outs, scratch, place=pltpu.VMEM):
    def run(*args):
        return pl.pallas_call(
            kernel,
            out_shape=[jax.ShapeDtypeStruct(shape, jnp.float32) for shape in outs],
            in_specs=[pl.BlockSpec(memory_space=place)] * len(args),
            out_specs=[pl.BlockSpec(memory_space=pltpu.VMEM)] * len(outs),
            scratch_shapes=scratch,
            compiler_params=pltpu.CompilerParams(vmem_limit_bytes=8 * 2**20),
        )(*args)

    return run


def chip_shards(velocity):
    bx, by, bz = velocity.shape[1:]
    chips = lax.axis_size("gy")
    length = bz * lax.axis_size("gz")
    low_type, wide_type = jnp.bfloat16, jnp.float32
    tables = [
        velocity_plane_table(bx, by),
        pair_plane_table(bx, by),
        line_table(length, ((3.0, False), (3.0, True), (6.0, False), (6.0, True))),
        line_table(length, ((12.0, False), (12.0, True), (6.0, False), (0.0, False))),
    ]
    tables = [jnp.asarray(table, low_type) for table in tables]
    shapes = [tables[0].shape, tables[1].shape, (bz, 128), (bz, 128)]
    (part,) = call(
        sums_kernel,
        [(ROWS + 3 * FACE, 128)],
        [pltpu.VMEM(velocity.shape, wide_type)]
        + [pltpu.VMEM(shape, low_type) for shape in shapes]
        + [pltpu.VMEM((8 * shapes[1][0], 128), wide_type), pltpu.SemaphoreType.DMA((7,))],
        pltpu.HBM,
    )(*[pltpu.with_memory_space_constraint(value, pltpu.HBM) for value in (velocity, *tables)])
    part = part + lax.ppermute(part, "gz", [(0, 1), (1, 0)])
    own = part[: ROWS + FACE]
    low = moved(part[ROWS + FACE : ROWS + 2 * FACE], "gx", -1)
    high = moved(part[ROWS + 2 * FACE :], "gx", 1)
    left = jnp.arange(128, dtype=jnp.int32)[None, :] < 64
    middle = jnp.zeros((ROWS - FACE, 128), wide_type)
    own = own + jnp.concatenate(
        [jnp.where(left, high, low), middle, jnp.where(left, low, high)], axis=0
    )

    sums = gathered_over(own, "gy")
    stacked, gram = call(
        features_kernel,
        [(128, 128), (56, 128)],
        [
            pltpu.VMEM((chips, ROWS + FACE, 128), wide_type),
            pltpu.VMEM((27 * chips, 128), wide_type),
            pltpu.VMEM((chips, 128, 128), wide_type),
        ],
    )(*sums)
    grams = gathered_over(gram, "gx")
    samples = (bx // 8) * (by // 8) * (length // 8)
    total = float(samples * lax.axis_size("gx") * chips)
    residual, coefficients = call(
        functools.partial(solve_kernel, total), [(6, 64), (6, 96)], [pltpu.VMEM((4, 56, 128), wide_type)]
    )(*grams, stacked)
    return (residual, coefficients.T)


def chip_form(mesh, velocity):
    shape = mesh.shape
    brick = (velocity.shape[1] // shape["gx"], velocity.shape[2] // shape["gy"])
    return (
        shape["gx"] == shape["gy"] == 4 and shape["gz"] == 2
        and brick == (16, 16) and velocity.shape[3] == 256
    )


def solution(mesh):
    in_specs = (P(None, "gx", "gy", "gz"),)
    out_specs = (P(None, ("gx", "gy", "gz")), P())

    def run(velocity):
        body = chip_shards if chip_form(mesh, velocity) else shards
        return jax.shard_map(
            body, mesh=mesh, in_specs=in_specs, out_specs=out_specs, check_vma=False
        )(velocity)

    return run
```

```python
import functools

import jax
import jax.numpy as jnp
import numpy as np
from jax import lax
from jax.experimental import pallas as pl
from jax.experimental.pallas import tpu as pltpu
from jax.sharding import PartitionSpec as P

PRECISE = lax.Precision.HIGHEST
INDEX_PAIRS = ((0, 0), (1, 1), (2, 2), (0, 1), (0, 2), (1, 2))
WIDTHS = (3.0, 6.0, 12.0)


def extended(block, sides, width):
    for axis, dim in sides:
        count = lax.axis_size(axis)
        forward = [(i, i + 1) for i in range(count - 1)]
        forward.append((count - 1, 0))
        backward = [(target, source) for source, target in forward]
        low = lax.ppermute(
            lax.slice_in_dim(block, block.shape[dim] - width, None, axis=dim), axis, forward
        )
        high = lax.ppermute(lax.slice_in_dim(block, 0, width, axis=dim), axis, backward)
        block = jnp.concatenate([low, block, high], axis=dim)
    return block


def window_table(combos):
    weights_table = np.zeros((len(combos), 16), np.float32)
    for row_index in range(len(combos)):
        box_width, offset = combos[row_index]
        low_edge = 7.5 + offset - box_width / 2.0
        high_edge = 7.5 + offset + box_width / 2.0
        for cell_index in range(16):
            cell_share = min(cell_index + 0.5, high_edge) - max(cell_index - 0.5, low_edge)
            weights_table[row_index, cell_index] = max(cell_share, 0.0) / box_width
    return weights_table


def velocity_combos():
    return [(box_width, offset) for box_width in WIDTHS for offset in (-2.0, 0.0, 2.0)]


def product_combos():
    return [(3.0, 0.0), (12.0, 0.0)]


def matrix_product(left_matrix, right_matrix):
    return [
        [
            left_matrix[i][0] * right_matrix[0][j]
            + left_matrix[i][1] * right_matrix[1][j]
            + left_matrix[i][2] * right_matrix[2][j]
            for j in range(3)
        ]
        for i in range(3)
    ]


def pick_pairs(matrix):
    return [matrix[i][j] for i, j in INDEX_PAIRS]


def build_rows(box_means, pair_means):
    feature_rows = []
    centre_values = []
    for width_index in range(3):
        middle = 3 * width_index + 1
        scaled = WIDTHS[width_index] ** 2 * 0.25

        def offset_value(component, direction, step_size):
            position_list = [middle, middle, middle]
            position_list[direction] = middle + step_size
            return box_means[component, position_list[0], position_list[1], position_list[2]]

        centre_values.append([box_means[i, middle, middle, middle] for i in range(3)])
        gradient = [
            [(offset_value(i, j, 1) - offset_value(i, j, -1)) * scaled for j in range(3)]
            for i in range(3)
        ]
        strain = [[(gradient[i][j] + gradient[j][i]) * 0.5 for j in range(3)] for i in range(3)]
        spin_part = [[(gradient[i][j] - gradient[j][i]) * 0.5 for j in range(3)] for i in range(3)]
        square_strain = matrix_product(strain, strain)
        first_order = matrix_product(strain, spin_part)
        second_order = matrix_product(spin_part, strain)
        commutator = [[first_order[i][j] - second_order[i][j] for j in range(3)] for i in range(3)]
        spin_square = matrix_product(spin_part, spin_part)
        magnitude = sum((strain[i][j] * strain[i][j] for i in range(3) for j in range(3)))
        feature_rows += (
            pick_pairs(strain)
            + pick_pairs(square_strain)
            + pick_pairs(commutator)
            + pick_pairs(spin_square)
        )
        feature_rows += [magnitude * entry for entry in pick_pairs(strain)]
    small_box = centre_values[0]
    large_box = centre_values[2]
    feature_rows += [
        pair_means[index, 0] - small_box[i] * small_box[j]
        for index, (i, j) in enumerate(INDEX_PAIRS)
    ]
    target_rows = [
        pair_means[index, 1] - large_box[i] * large_box[j]
        for index, (i, j) in enumerate(INDEX_PAIRS)
    ]
    return (jnp.stack(feature_rows), jnp.stack(target_rows))


def solve_fit(gram_matrix, sample_total):
    scales = jnp.sqrt(jnp.diagonal(gram_matrix) / sample_total + 1e-06)
    feature_scale = scales[:96]
    normal = gram_matrix[:96, :96] / (
        sample_total * feature_scale[:, None] * feature_scale[None, :]
    ) + 0.1 * jnp.eye(96, dtype=jnp.float32)
    target_side = gram_matrix[:96, 96:] / (sample_total * feature_scale[:, None])
    factor = jnp.linalg.cholesky(normal)
    solved = jax.scipy.linalg.cho_solve((factor, True), target_side)
    return (solved / feature_scale[:, None], scales[96:])


def axis_weights(length, weights_table):
    sample_count = length // 8
    combo_count = weights_table.shape[0]
    full_table = np.zeros((sample_count * combo_count, length + 8), np.float32)
    for sample_index in range(sample_count):
        full_table[
            sample_index * combo_count : (sample_index + 1) * combo_count,
            8 * sample_index : 8 * sample_index + 16,
        ] = weights_table
    return jnp.asarray(full_table)


def windowed(wide_field, weights_table):
    along_z = jnp.einsum(
        "cxyz,kz->cxyk",
        wide_field,
        axis_weights(wide_field.shape[3] - 8, weights_table),
        precision=PRECISE,
    )
    along_y = jnp.einsum(
        "cxyk,jy->cxjk",
        along_z,
        axis_weights(wide_field.shape[2] - 8, weights_table),
        precision=PRECISE,
    )
    return jnp.einsum(
        "cxjk,ix->cijk",
        along_y,
        axis_weights(wide_field.shape[1] - 8, weights_table),
        precision=PRECISE,
    )


def shards(velocity):
    rounded = velocity.astype(jnp.bfloat16)
    padded = extended(rounded, (("gx", 1), ("gy", 2), ("gz", 3)), 4)
    wide_field = padded.astype(jnp.float32)
    count_x = velocity.shape[1] // 8
    count_y = velocity.shape[2] // 8
    count_z = velocity.shape[3] // 8
    samples = count_x * count_y * count_z
    box_means = windowed(wide_field, window_table(velocity_combos()))
    box_means = box_means.reshape(3, count_x, 9, count_y, 9, count_z, 9)
    box_means = jnp.transpose(box_means, (0, 2, 4, 6, 1, 3, 5)).reshape(3, 9, 9, 9, samples)
    pair_field = jnp.stack([wide_field[i] * wide_field[j] for i, j in INDEX_PAIRS])
    pair_means = windowed(pair_field, window_table(product_combos())).reshape(
        6, count_x, 2, count_y, 2, count_z, 2
    )
    pair_means = jnp.stack(
        [pair_means[:, :, 0, :, 0, :, 0], pair_means[:, :, 1, :, 1, :, 1]], axis=1
    )
    pair_means = pair_means.reshape(6, 2, samples)
    features, targets = build_rows(box_means, pair_means)
    stacked = jnp.concatenate([features, targets], axis=0)
    local_gram = jnp.dot(stacked, stacked.T, precision=PRECISE, preferred_element_type=jnp.float32)
    gram_matrix = lax.psum(local_gram, ("gx", "gy", "gz"))
    sample_total = float(samples * lax.axis_size("gx") * lax.axis_size("gy") * lax.axis_size("gz"))
    coefficients, target_scale = solve_fit(gram_matrix, sample_total)
    predicted = jnp.dot(
        coefficients.T, features, precision=PRECISE, preferred_element_type=jnp.float32
    )
    residual = (targets - predicted) / target_scale[:, None]
    return (residual, coefficients)


OWN = ((0, 0), (0, 1), (1, 0), (1, 1))
FACE_LOW = ((-1, -1), (-1, 2), (-1, 0), (-1, 1))
FACE_HIGH = ((2, 0), (2, 1), (2, -1), (2, 2))
FACE_Y = ((1, -1), (1, 2), (0, -1), (0, 2))
ROWS, FACE = 48, 24


def share(centre, width, cell):
    part = min(cell + 0.5, centre + width / 2) - max(cell - 0.5, centre - width / 2)
    return max(part, 0.0)


def window(length, width, sample, difference, turns=(0,)):
    total = np.zeros(length)
    for shift, sign in ((2.0, 1.0), (-2.0, -1.0)) if difference else ((0.0, 1.0),):
        for cell in range(length):
            for turn in turns:
                total[cell] += sign * share(
                    8 * sample + 3.5 + shift, width, cell + turn * length
                )
    return total


def plane_row(bx, by, place, width, direction):
    return np.outer(
        window(bx, width, place[0], direction == 0), window(by, width, place[1], direction == 1)
    ).reshape(-1)


def velocity_plane_table(bx, by):
    none = np.zeros(bx * by)
    rows = []
    for place in OWN:
        three = [plane_row(bx, by, place, 3.0, k) for k in (0, 1, 2)]
        six = [plane_row(bx, by, place, 6.0, k) for k in (0, 1, 2)]
        rows += three + [three[2]] + six + [none]
    for places in (OWN, FACE_LOW, FACE_HIGH, FACE_Y):
        for place in places:
            twelve = [plane_row(bx, by, place, 12.0, k) for k in (0, 1, 2)]
            along = {FACE_LOW: 0, FACE_HIGH: 0, FACE_Y: 1}.get(places)
            last = none if along is None else plane_row(bx, by, place, 6.0, along)
            rows += twelve + [twelve[2], last, none, none, none]
    return np.stack(rows)


def pair_plane_table(bx, by):
    rows = [plane_row(bx, by, place, 3.0, 2) for place in OWN]
    for places in (OWN, FACE_LOW, FACE_HIGH, FACE_Y):
        rows += [plane_row(bx, by, place, 12.0, 2) for place in places]
    while len(rows) % 16:
        rows.append(np.zeros(bx * by))
    return np.stack(rows)


def line_table(length, blocks):
    columns = []
    for width, difference in blocks:
        for sample in range(length // 8):
            if width:
                columns.append(window(length, width, sample, difference, (-1, 0, 1)))
            else:
                columns.append(np.zeros(length))
    return np.stack(columns, axis=1)


def three_parts(value):
    high = value.astype(jnp.bfloat16)
    rest = value - high.astype(jnp.float32)
    middle = rest.astype(jnp.bfloat16)
    low = (rest - middle.astype(jnp.float32)).astype(jnp.bfloat16)
    return high, middle, low


def mxu(left, right):
    return jnp.dot(left, right, preferred_element_type=jnp.float32)


def sums_kernel(x_hbm, wv_hbm, wp_hbm, la_hbm, lb_hbm, out_ref, x_ref, wv, wp, la, lb, pair_ref, sems):
    core = lax.axis_index("gz")
    cells = x_ref.shape[1] * x_ref.shape[2]
    length = x_ref.shape[3]
    begin = pl.multiple_of(core * length, length)
    copies = [pltpu.make_async_copy(wv_hbm, wv, sems.at[0])]
    copies += [pltpu.make_async_copy(x_hbm.at[c], x_ref.at[c], sems.at[1 + c]) for c in range(3)]
    copies += [pltpu.make_async_copy(wp_hbm, wp, sems.at[4])]
    copies += [pltpu.make_async_copy(la_hbm.at[pl.ds(begin, length)], la, sems.at[5])]
    copies += [pltpu.make_async_copy(lb_hbm.at[pl.ds(begin, length)], lb, sems.at[6])]
    for copy in copies:
        copy.start()
    rows = lax.broadcasted_iota(jnp.int32, (8, 128), 0)
    lanes = lax.broadcasted_iota(jnp.int32, (8, 128), 1) // 32
    pair_ref[...] = jnp.zeros(pair_ref.shape, jnp.float32)

    def gathered(groups, blocks):
        total = jnp.zeros((8, 128), jnp.float32)
        for place in range(4):
            base = groups[8 * place : 8 * place + 8]
            merged = pltpu.roll(base, 32 * place, 1) if place else base
            for block, chosen in blocks:
                hit = rows == chosen[0]
                for row in chosen[1:]:
                    hit = hit | (rows == row)
                turn = 32 * (place - block) % 128
                merged = jnp.where(hit, pltpu.roll(base, turn, 1) if turn else base, merged)
            total = jnp.where(lanes == place, merged, total)
        return total

    for copy in copies:
        copy.wait()
    fields = [x_ref[c].reshape(cells, length).astype(jnp.bfloat16) for c in range(3)]
    planes = [mxu(wv[...], field) for field in fields]
    wide = [field.astype(jnp.float32) for field in fields]
    count = wp.shape[0]
    weights = jnp.concatenate([wp[...], wp[...]], axis=1)
    for pair, (i, j) in enumerate(INDEX_PAIRS):
        product = wide[i] * wide[j]
        high = product.astype(jnp.bfloat16)
        low = (product - high.astype(jnp.float32)).astype(jnp.bfloat16)
        pair_ref[pl.ds(pair, count, stride=8), :] = mxu(
            weights, jnp.concatenate([high, low], axis=0)
        )

    def along_line(value, line):
        high, middle, low = three_parts(value)
        return mxu(
            jnp.concatenate([high, middle], axis=1), jnp.concatenate([line, line], axis=0)
        ) + mxu(low, line)

    narrow = along_line(
        jnp.concatenate([plane[:32] for plane in planes] + [pair_ref[pl.ds(0, 32), :]], axis=0),
        la[...],
    )
    broad = along_line(
        jnp.concatenate([plane[32:] for plane in planes] + [pair_ref[pl.ds(32, 128), :]], axis=0),
        lb[...],
    )
    for c in range(3):
        value = gathered(narrow[32 * c : 32 * c + 32], ((1, (2,)), (2, (4, 5)), (3, (6,))))
        out_ref[pl.ds(27 + 3 * c, 3), :] = value[0:3]
        out_ref[pl.ds(36 + c, 1), :] = value[3:4]
        out_ref[pl.ds(12 + c, 1), :] = value[4:5]
        out_ref[pl.ds(21 + c, 1), :] = value[5:6]
        out_ref[pl.ds(24 + c, 1), :] = value[6:7]
        for part in range(4):
            at = 128 * c + 32 * part
            base = (0, ROWS + FACE, ROWS + 2 * FACE, ROWS)[part]
            blocks = ((1, (2,)), (2, (4,))) if part else ((1, (2,)),)
            value = gathered(broad[at : at + 32], blocks)
            out_ref[pl.ds(base + 3 * c, 3), :] = value[0:3]
            out_ref[pl.ds(base + 9 + c, 1), :] = value[3:4]
            if part:
                live, still = (12, 21) if part < 3 else (21, 12)
                out_ref[pl.ds(base + live + c, 1), :] = value[4:5]
                out_ref[pl.ds(base + still + c, 1), :] = jnp.zeros((1, 128), jnp.float32)
    out_ref[pl.ds(39, 6), :] = gathered(narrow[96:128], ())[:6]
    out_ref[pl.ds(45, 3), :] = jnp.zeros((3, 128), jnp.float32)
    for part in range(4):
        base = (0, ROWS + FACE, ROWS + 2 * FACE, ROWS)[part]
        out_ref[pl.ds(base + 15, 6), :] = gathered(broad[384 + 32 * part : 416 + 32 * part], ())[:6]


def features_kernel(own_ref, one_ref, swap_ref, both_ref, z_out, gram_ref, b_ref, a_ref, z_ref):
    mine = lax.axis_index("gy")
    chips = b_ref.shape[0]
    in_order(b_ref, mine, (own_ref, one_ref, swap_ref, both_ref), False)
    lane = lax.broadcasted_iota(jnp.int32, (FACE, 128), 1)
    upper = (lane // 32) % 2 == 1
    z_ref[:, 96:, :] = jnp.zeros((chips, 32, 128), jnp.float32)
    for chip in range(chips):
        after = pltpu.roll(b_ref[(chip + 1) % chips, ROWS:, :], 96, 1)
        before = pltpu.roll(b_ref[(chip - 1) % chips, ROWS:, :], 32, 1)
        sums = b_ref[chip, :FACE, :] + jnp.where(upper, after, before)
        base = 27 * chip
        a_ref[pl.ds(base, 9), :] = b_ref[chip, 27:36, :]
        a_ref[pl.ds(base + 9, 3, stride=3), :] = sums[12:15]
        a_ref[pl.ds(base + 10, 3, stride=3), :] = sums[21:24]
        a_ref[pl.ds(base + 11, 3, stride=3), :] = b_ref[chip, 24:27, :]
        a_ref[pl.ds(base + 18, 9), :] = sums[0:9]
        for at, centres, products, width in (
            (90, b_ref[chip, 36:39, :], b_ref[chip, 39:45, :], 3.0),
            (96, sums[9:12], sums[15:21], 12.0),
        ):
            means = [centres[c : c + 1] * (1.0 / width**3) for c in range(3)]
            for pair, (i, j) in enumerate(INDEX_PAIRS):
                z_ref[chip, pl.ds(at + pair, 1), :] = (
                    products[pair : pair + 1] * (1.0 / width**3) - means[i] * means[j]
                )
    total = 3 * chips
    width = lax.broadcasted_iota(jnp.int32, (total, 128), 0) % 3
    factor = jnp.where(width == 0, 1.0 / 12.0, jnp.where(width == 1, 1.0 / 24.0, 1.0 / 48.0))
    grad = [
        [a_ref[pl.ds(3 * i + j, total, stride=9), :] * factor for j in range(3)] for i in range(3)
    ]
    strain = [[None] * 3 for _ in range(3)]
    spin = [[None] * 3 for _ in range(3)]
    for i in range(3):
        for j in range(i, 3):
            strain[i][j] = strain[j][i] = (grad[i][j] + grad[j][i]) * 0.5
            if i != j:
                spin[i][j] = (grad[i][j] - grad[j][i]) * 0.5
                spin[j][i] = (grad[j][i] - grad[i][j]) * 0.5

    def entry(left, right, i, j):
        terms = [
            left[i][k] * right[k][j]
            for k in range(3)
            if left[i][k] is not None and right[k][j] is not None
        ]
        return sum(terms[1:], terms[0])

    squares = [strain[i][j] * strain[i][j] for i in range(3) for j in range(3)]
    magnitude = sum(squares[1:], squares[0])
    columns = [strain[i][j] for i, j in INDEX_PAIRS]
    columns += [entry(strain, strain, i, j) for i, j in INDEX_PAIRS]
    columns += [entry(strain, spin, i, j) - entry(spin, strain, i, j) for i, j in INDEX_PAIRS]
    columns += [entry(spin, spin, i, j) for i, j in INDEX_PAIRS]
    columns += [magnitude * strain[i][j] for i, j in INDEX_PAIRS]
    for index, column in enumerate(columns):
        for chip in range(chips):
            z_ref[chip, pl.ds(index, 3, stride=30), :] = column[3 * chip : 3 * chip + 3]
    z_out[...] = z_ref[mine]
    stacked = jnp.concatenate([z_ref[chip] for chip in range(chips)], axis=1)
    gram = lax.dot_general(
        stacked[:104],
        stacked,
        (((1,), (1,)), ((), ())),
        precision=PRECISE,
        preferred_element_type=jnp.float32,
    )
    rows = lax.broadcasted_iota(jnp.int32, (8, 128), 0)
    lane = lax.broadcasted_iota(jnp.int32, (8, 128), 1)
    gram_ref[pl.ds(0, 8), :] = gram[:8]
    for p in range(1, 7):
        lower = pltpu.roll(gram[48 + 8 * p : 56 + 8 * p], 72, 1)
        gram_ref[pl.ds(8 * p, 8), :] = jnp.where(
            lane >= rows + 8 * p, gram[8 * p : 8 * p + 8], lower
        )


def solve_kernel(total, own_ref, one_ref, swap_ref, both_ref, z_ref, res_ref, coef_ref, g_ref):
    core = lax.axis_index("gz")
    in_order(g_ref, lax.axis_index("gx"), (own_ref, one_ref, swap_ref, both_ref), True)
    packed = [
        (g_ref[0, pl.ds(8 * i, 8), :] + g_ref[1, pl.ds(8 * i, 8), :])
        + (g_ref[2, pl.ds(8 * i, 8), :] + g_ref[3, pl.ds(8 * i, 8), :])
        for i in range(7)
    ]
    one = jnp.where(core >= 0, 1.0, 2.0)
    count, group = 12, 2
    rows = lax.broadcasted_iota(jnp.int32, (8, 128), 0)
    lane = lax.broadcasted_iota(jnp.int32, (8, 128), 1)
    half = []
    for i in range(count + 1):
        if i < 7:
            value = packed[i]
            half.append(jnp.where(lane >= rows + 8 * i, value, 0.0))
        else:
            value = pltpu.roll(packed[i - 6], 56, 1)
            half.append(jnp.where((lane >= 56) & (lane <= rows + 8 * i), value, 0.0))
    blank = [jnp.zeros((8, 128), jnp.float32)]
    other = jnp.transpose(jnp.concatenate(half + blank * (15 - count), axis=0))
    block = []
    for i in range(count + 1):
        value = half[i]
        ridge = value + 0.1 * (value + total * 1e-06) if i < count else value
        value = value + other[8 * i : 8 * i + 8]
        block.append(jnp.where(lane == rows + 8 * i, ridge, value))
    diag = jnp.sum(jnp.where(lane == rows + 96, block[count], 0.0), axis=1, keepdims=True)
    scale = jnp.broadcast_to(jnp.sqrt(diag / total + 1e-06), (8, 128))

    def spread(value, column):
        return jnp.broadcast_to(value[:, column : column + 1], (8, 128))

    def row_of(parts, row):
        return jnp.broadcast_to(parts[row // 8][row % 8 : row % 8 + 1, :], (8, 128))

    for start in range(0, count, group):
        size = 8 * group
        first = 8 * start
        near = range(start + group, min(start + 2 * group, count + 1))
        far = range(start + 2 * group, count + 1)
        square = [[spread(block[start + p], first + m) * one for p in range(group)] for m in range(size)]
        below = {i: [spread(block[i], first + m) for m in range(size)] for i in near}
        inside = (lane >= first) & (lane < first + size)
        panel = []
        for p in range(group):
            unit = (lane == rows + first + 8 * p).astype(jnp.float32)
            panel.append(jnp.where(inside, -unit, block[start + p]))
        inverses = []
        for m in range(size):
            inverses.append(1.0 / row_of(square[m], m))
            factor = [
                jnp.where(rows == m - 8 * p, 0.0, square[m][p]) if m // 8 == p else square[m][p]
                for p in range(group)
            ]
            for k in range(m + 1, size):
                line = row_of(square[k], m) * inverses[m]
                square[k] = [square[k][p] - factor[p] * line for p in range(group)]
            line = row_of(panel, m) * inverses[m]
            panel = [panel[p] - factor[p] * line for p in range(group)]
        lines = [row_of(panel, m) * inverses[m] for m in range(size)]
        for i in near:
            terms = [below[i][m] * lines[m] for m in range(size)]
            while len(terms) > 1:
                terms = [terms[t] + terms[t + 1] for t in range(0, len(terms), 2)]
            block[i] = jnp.where(inside, 0.0, block[i]) - terms[0]
        if far:
            scaled = []
            for p in range(group):
                inverse = inverses[8 * p]
                for row in range(1, 8):
                    inverse = jnp.where(rows == row, inverses[8 * p + row], inverse)
                scaled.append(panel[p] * inverse)
            blank = [jnp.zeros((8, 128), jnp.float32)]
            right = jnp.concatenate(blank * start + scaled + blank * (16 - group - start), axis=0)
            left = jnp.concatenate([jnp.where(inside, block[i], 0.0) for i in far], axis=0)
            change = jnp.dot(left, right, precision=PRECISE, preferred_element_type=jnp.float32)
            for at, i in enumerate(far):
                block[i] = jnp.where(inside, 0.0, block[i]) - change[8 * at : 8 * at + 8]
    answer = jnp.where(lane < 96, block[count], 0.0)
    coef_ref[...] = answer[:6, :96]
    predicted = jnp.dot(answer, z_ref[...], precision=PRECISE, preferred_element_type=jnp.float32)
    residual = (z_ref[pl.ds(96, 8), :] - predicted) / scale
    picked = jnp.zeros((8, 128), jnp.float32)
    for place in range(4):
        even = pltpu.roll(residual, (128 - 16 * place) % 128, 1) if place else residual
        odd = pltpu.roll(residual, 112 - 16 * place, 1)
        picked = jnp.where(lane // 16 == place, jnp.where(core == 0, even, odd), picked)
    res_ref[...] = picked[:6, :64]


def crosswise(value, axis, target):
    pairs = []
    for chip in range(lax.axis_size(axis)):
        for core in range(2):
            pairs.append((2 * chip + core, 2 * target(chip) + 1 - core))
    return lax.ppermute(value, (axis, "gz"), pairs)


def moved(value, axis, step):
    size = lax.axis_size(axis)
    return crosswise(value, axis, lambda chip: (chip + step) % size)


def gathered_over(value, axis, straight):
    pairs = []
    for chip in range(lax.axis_size(axis)):
        if straight:
            pairs += [(2 * chip, 2 * (chip ^ 1)), (2 * chip + 1, 2 * (chip ^ 2) + 1)]
        else:
            pairs += [(2 * chip, 2 * (chip ^ 1) + 1), (2 * chip + 1, 2 * (chip ^ 2))]
    both = crosswise(value, axis, lambda chip: chip ^ 3)
    one = lax.ppermute(value, (axis, "gz"), pairs)
    return value, one, lax.ppermute(one, "gz", [(0, 1), (1, 0)]), both


def in_order(target_ref, mine, refs, straight):
    core = lax.axis_index("gz")
    first = 1 + core if straight else 2 - core
    own_ref, one_ref, swap_ref, both_ref = refs
    target_ref[mine] = own_ref[...]
    target_ref[jnp.bitwise_xor(mine, first)] = one_ref[...]
    target_ref[jnp.bitwise_xor(mine, 3 - first)] = swap_ref[...]
    target_ref[jnp.bitwise_xor(mine, 3)] = both_ref[...]


def call(kernel, outs, scratch, place=pltpu.VMEM):
    def run(*args):
        return pl.pallas_call(
            kernel,
            out_shape=[jax.ShapeDtypeStruct(shape, jnp.float32) for shape in outs],
            in_specs=[pl.BlockSpec(memory_space=place)] * len(args),
            out_specs=[pl.BlockSpec(memory_space=pltpu.VMEM)] * len(outs),
            scratch_shapes=scratch,
            compiler_params=pltpu.CompilerParams(vmem_limit_bytes=8 * 2**20),
        )(*args)

    return run


def chip_shards(velocity):
    bx, by, bz = velocity.shape[1:]
    chips = lax.axis_size("gy")
    length = bz * lax.axis_size("gz")
    low_type, wide_type = jnp.bfloat16, jnp.float32
    tables = [
        velocity_plane_table(bx, by),
        pair_plane_table(bx, by),
        line_table(length, ((3.0, False), (3.0, True), (6.0, False), (6.0, True))),
        line_table(length, ((12.0, False), (12.0, True), (6.0, False), (0.0, False))),
    ]
    tables = [jnp.asarray(table, low_type) for table in tables]
    shapes = [tables[0].shape, tables[1].shape, (bz, 128), (bz, 128)]
    (part,) = call(
        sums_kernel,
        [(ROWS + 3 * FACE, 128)],
        [pltpu.VMEM(velocity.shape, wide_type)]
        + [pltpu.VMEM(shape, low_type) for shape in shapes]
        + [pltpu.VMEM((8 * shapes[1][0], 128), wide_type), pltpu.SemaphoreType.DMA((7,))],
        pltpu.HBM,
    )(*[pltpu.with_memory_space_constraint(value, pltpu.HBM) for value in (velocity, *tables)])
    part = part + lax.ppermute(part, "gz", [(0, 1), (1, 0)])
    own = part[: ROWS + FACE]
    low = moved(part[ROWS + FACE : ROWS + 2 * FACE], "gx", -1)
    high = moved(part[ROWS + 2 * FACE :], "gx", 1)
    left = jnp.arange(128, dtype=jnp.int32)[None, :] < 64
    middle = jnp.zeros((ROWS - FACE, 128), wide_type)
    own = own + jnp.concatenate(
        [jnp.where(left, high, low), middle, jnp.where(left, low, high)], axis=0
    )

    sums = gathered_over(own, "gy", False)
    stacked, gram = call(
        features_kernel,
        [(128, 128), (56, 128)],
        [
            pltpu.VMEM((chips, ROWS + FACE, 128), wide_type),
            pltpu.VMEM((27 * chips, 128), wide_type),
            pltpu.VMEM((chips, 128, 128), wide_type),
        ],
    )(*sums)
    grams = gathered_over(gram, "gx", True)
    samples = (bx // 8) * (by // 8) * (length // 8)
    total = float(samples * lax.axis_size("gx") * chips)
    residual, coefficients = call(
        functools.partial(solve_kernel, total), [(6, 64), (6, 96)], [pltpu.VMEM((4, 56, 128), wide_type)]
    )(*grams, stacked)
    return (residual, coefficients.T)


def chip_form(mesh, velocity):
    shape = mesh.shape
    brick = (velocity.shape[1] // shape["gx"], velocity.shape[2] // shape["gy"])
    return (
        shape["gx"] == shape["gy"] == 4 and shape["gz"] == 2
        and brick == (16, 16) and velocity.shape[3] == 256
    )


def solution(mesh):
    in_specs = (P(None, "gx", "gy", "gz"),)
    out_specs = (P(None, ("gx", "gy", "gz")), P())

    def run(velocity):
        body = chip_shards if chip_form(mesh, velocity) else shards
        return jax.shard_map(
            body, mesh=mesh, in_specs=in_specs, out_specs=out_specs, check_vma=False
        )(velocity)

    return run
```

```python
import functools

import jax
import jax.numpy as jnp
import numpy as np
from jax import lax
from jax.experimental import pallas as pl
from jax.experimental.pallas import tpu as pltpu
from jax.sharding import PartitionSpec as P

PRECISE = lax.Precision.HIGHEST
INDEX_PAIRS = ((0, 0), (1, 1), (2, 2), (0, 1), (0, 2), (1, 2))
WIDTHS = (3.0, 6.0, 12.0)


def extended(block, sides, width):
    for axis, dim in sides:
        count = lax.axis_size(axis)
        forward = [(i, i + 1) for i in range(count - 1)]
        forward.append((count - 1, 0))
        backward = [(target, source) for source, target in forward]
        low = lax.ppermute(
            lax.slice_in_dim(block, block.shape[dim] - width, None, axis=dim), axis, forward
        )
        high = lax.ppermute(lax.slice_in_dim(block, 0, width, axis=dim), axis, backward)
        block = jnp.concatenate([low, block, high], axis=dim)
    return block


def window_table(combos):
    weights_table = np.zeros((len(combos), 16), np.float32)
    for row_index in range(len(combos)):
        box_width, offset = combos[row_index]
        low_edge = 7.5 + offset - box_width / 2.0
        high_edge = 7.5 + offset + box_width / 2.0
        for cell_index in range(16):
            cell_share = min(cell_index + 0.5, high_edge) - max(cell_index - 0.5, low_edge)
            weights_table[row_index, cell_index] = max(cell_share, 0.0) / box_width
    return weights_table


def velocity_combos():
    return [(box_width, offset) for box_width in WIDTHS for offset in (-2.0, 0.0, 2.0)]


def product_combos():
    return [(3.0, 0.0), (12.0, 0.0)]


def matrix_product(left_matrix, right_matrix):
    return [
        [
            left_matrix[i][0] * right_matrix[0][j]
            + left_matrix[i][1] * right_matrix[1][j]
            + left_matrix[i][2] * right_matrix[2][j]
            for j in range(3)
        ]
        for i in range(3)
    ]


def pick_pairs(matrix):
    return [matrix[i][j] for i, j in INDEX_PAIRS]


def build_rows(box_means, pair_means):
    feature_rows = []
    centre_values = []
    for width_index in range(3):
        middle = 3 * width_index + 1
        scaled = WIDTHS[width_index] ** 2 * 0.25

        def offset_value(component, direction, step_size):
            position_list = [middle, middle, middle]
            position_list[direction] = middle + step_size
            return box_means[component, position_list[0], position_list[1], position_list[2]]

        centre_values.append([box_means[i, middle, middle, middle] for i in range(3)])
        gradient = [
            [(offset_value(i, j, 1) - offset_value(i, j, -1)) * scaled for j in range(3)]
            for i in range(3)
        ]
        strain = [[(gradient[i][j] + gradient[j][i]) * 0.5 for j in range(3)] for i in range(3)]
        spin_part = [[(gradient[i][j] - gradient[j][i]) * 0.5 for j in range(3)] for i in range(3)]
        square_strain = matrix_product(strain, strain)
        first_order = matrix_product(strain, spin_part)
        second_order = matrix_product(spin_part, strain)
        commutator = [[first_order[i][j] - second_order[i][j] for j in range(3)] for i in range(3)]
        spin_square = matrix_product(spin_part, spin_part)
        magnitude = sum((strain[i][j] * strain[i][j] for i in range(3) for j in range(3)))
        feature_rows += (
            pick_pairs(strain)
            + pick_pairs(square_strain)
            + pick_pairs(commutator)
            + pick_pairs(spin_square)
        )
        feature_rows += [magnitude * entry for entry in pick_pairs(strain)]
    small_box = centre_values[0]
    large_box = centre_values[2]
    feature_rows += [
        pair_means[index, 0] - small_box[i] * small_box[j]
        for index, (i, j) in enumerate(INDEX_PAIRS)
    ]
    target_rows = [
        pair_means[index, 1] - large_box[i] * large_box[j]
        for index, (i, j) in enumerate(INDEX_PAIRS)
    ]
    return (jnp.stack(feature_rows), jnp.stack(target_rows))


def solve_fit(gram_matrix, sample_total):
    scales = jnp.sqrt(jnp.diagonal(gram_matrix) / sample_total + 1e-06)
    feature_scale = scales[:96]
    normal = gram_matrix[:96, :96] / (
        sample_total * feature_scale[:, None] * feature_scale[None, :]
    ) + 0.1 * jnp.eye(96, dtype=jnp.float32)
    target_side = gram_matrix[:96, 96:] / (sample_total * feature_scale[:, None])
    factor = jnp.linalg.cholesky(normal)
    solved = jax.scipy.linalg.cho_solve((factor, True), target_side)
    return (solved / feature_scale[:, None], scales[96:])


def axis_weights(length, weights_table):
    sample_count = length // 8
    combo_count = weights_table.shape[0]
    full_table = np.zeros((sample_count * combo_count, length + 8), np.float32)
    for sample_index in range(sample_count):
        full_table[
            sample_index * combo_count : (sample_index + 1) * combo_count,
            8 * sample_index : 8 * sample_index + 16,
        ] = weights_table
    return jnp.asarray(full_table)


def windowed(wide_field, weights_table):
    along_z = jnp.einsum(
        "cxyz,kz->cxyk",
        wide_field,
        axis_weights(wide_field.shape[3] - 8, weights_table),
        precision=PRECISE,
    )
    along_y = jnp.einsum(
        "cxyk,jy->cxjk",
        along_z,
        axis_weights(wide_field.shape[2] - 8, weights_table),
        precision=PRECISE,
    )
    return jnp.einsum(
        "cxjk,ix->cijk",
        along_y,
        axis_weights(wide_field.shape[1] - 8, weights_table),
        precision=PRECISE,
    )


def shards(velocity):
    rounded = velocity.astype(jnp.bfloat16)
    padded = extended(rounded, (("gx", 1), ("gy", 2), ("gz", 3)), 4)
    wide_field = padded.astype(jnp.float32)
    count_x = velocity.shape[1] // 8
    count_y = velocity.shape[2] // 8
    count_z = velocity.shape[3] // 8
    samples = count_x * count_y * count_z
    box_means = windowed(wide_field, window_table(velocity_combos()))
    box_means = box_means.reshape(3, count_x, 9, count_y, 9, count_z, 9)
    box_means = jnp.transpose(box_means, (0, 2, 4, 6, 1, 3, 5)).reshape(3, 9, 9, 9, samples)
    pair_field = jnp.stack([wide_field[i] * wide_field[j] for i, j in INDEX_PAIRS])
    pair_means = windowed(pair_field, window_table(product_combos())).reshape(
        6, count_x, 2, count_y, 2, count_z, 2
    )
    pair_means = jnp.stack(
        [pair_means[:, :, 0, :, 0, :, 0], pair_means[:, :, 1, :, 1, :, 1]], axis=1
    )
    pair_means = pair_means.reshape(6, 2, samples)
    features, targets = build_rows(box_means, pair_means)
    stacked = jnp.concatenate([features, targets], axis=0)
    local_gram = jnp.dot(stacked, stacked.T, precision=PRECISE, preferred_element_type=jnp.float32)
    gram_matrix = lax.psum(local_gram, ("gx", "gy", "gz"))
    sample_total = float(samples * lax.axis_size("gx") * lax.axis_size("gy") * lax.axis_size("gz"))
    coefficients, target_scale = solve_fit(gram_matrix, sample_total)
    predicted = jnp.dot(
        coefficients.T, features, precision=PRECISE, preferred_element_type=jnp.float32
    )
    residual = (targets - predicted) / target_scale[:, None]
    return (residual, coefficients)


OWN = ((0, 0), (0, 1), (1, 0), (1, 1))
FACE_LOW = ((-1, -1), (-1, 2), (-1, 0), (-1, 1))
FACE_HIGH = ((2, 0), (2, 1), (2, -1), (2, 2))
FACE_Y = ((1, -1), (1, 2), (0, -1), (0, 2))
ROWS, FACE = 48, 24


def share(centre, width, cell):
    part = min(cell + 0.5, centre + width / 2) - max(cell - 0.5, centre - width / 2)
    return max(part, 0.0)


def window(length, width, sample, difference, turns=(0,)):
    total = np.zeros(length)
    for shift, sign in ((2.0, 1.0), (-2.0, -1.0)) if difference else ((0.0, 1.0),):
        for cell in range(length):
            for turn in turns:
                total[cell] += sign * share(
                    8 * sample + 3.5 + shift, width, cell + turn * length
                )
    return total


def plane_row(bx, by, place, width, direction):
    return np.outer(
        window(bx, width, place[0], direction == 0), window(by, width, place[1], direction == 1)
    ).reshape(-1)


def velocity_plane_table(bx, by):
    none = np.zeros(bx * by)
    rows = []
    for place in OWN:
        three = [plane_row(bx, by, place, 3.0, k) for k in (0, 1, 2)]
        six = [plane_row(bx, by, place, 6.0, k) for k in (0, 1, 2)]
        rows += three + [three[2]] + six + [none]
    for places in (OWN, FACE_LOW, FACE_HIGH, FACE_Y):
        for place in places:
            twelve = [plane_row(bx, by, place, 12.0, k) for k in (0, 1, 2)]
            along = {FACE_LOW: 0, FACE_HIGH: 0, FACE_Y: 1}.get(places)
            last = none if along is None else plane_row(bx, by, place, 6.0, along)
            rows += twelve + [twelve[2], last, none, none, none]
    return np.stack(rows)


def pair_plane_table(bx, by):
    rows = [plane_row(bx, by, place, 3.0, 2) for place in OWN]
    for places in (OWN, FACE_LOW, FACE_HIGH, FACE_Y):
        rows += [plane_row(bx, by, place, 12.0, 2) for place in places]
    while len(rows) % 16:
        rows.append(np.zeros(bx * by))
    return np.stack(rows)


def line_table(length, blocks):
    columns = []
    for width, difference in blocks:
        for sample in range(length // 8):
            if width:
                columns.append(window(length, width, sample, difference, (-1, 0, 1)))
            else:
                columns.append(np.zeros(length))
    return np.stack(columns, axis=1)


def three_parts(value):
    high = value.astype(jnp.bfloat16)
    rest = value - high.astype(jnp.float32)
    middle = rest.astype(jnp.bfloat16)
    low = (rest - middle.astype(jnp.float32)).astype(jnp.bfloat16)
    return high, middle, low


def mxu(left, right):
    return jnp.dot(left, right, preferred_element_type=jnp.float32)


def sums_kernel(x_hbm, wv_hbm, wp_hbm, la_hbm, lb_hbm, out_ref, x_ref, wv, wp, la, lb, pair_ref, sems):
    core = lax.axis_index("gz")
    cells = x_ref.shape[1] * x_ref.shape[2]
    length = x_ref.shape[3]
    begin = pl.multiple_of(core * length, length)
    copies = [pltpu.make_async_copy(wv_hbm, wv, sems.at[0])]
    copies += [pltpu.make_async_copy(x_hbm.at[c], x_ref.at[c], sems.at[1 + c]) for c in range(3)]
    copies += [pltpu.make_async_copy(wp_hbm, wp, sems.at[4])]
    copies += [pltpu.make_async_copy(la_hbm.at[pl.ds(begin, length)], la, sems.at[5])]
    copies += [pltpu.make_async_copy(lb_hbm.at[pl.ds(begin, length)], lb, sems.at[6])]
    for copy in copies[1:4] + copies[:1] + copies[4:]:
        copy.start()
    rows = lax.broadcasted_iota(jnp.int32, (8, 128), 0)
    lanes = lax.broadcasted_iota(jnp.int32, (8, 128), 1) // 32
    pair_ref[...] = jnp.zeros(pair_ref.shape, jnp.float32)

    def gathered(groups, blocks):
        total = jnp.zeros((8, 128), jnp.float32)
        for place in range(4):
            base = groups[8 * place : 8 * place + 8]
            merged = pltpu.roll(base, 32 * place, 1) if place else base
            for block, chosen in blocks:
                hit = rows == chosen[0]
                for row in chosen[1:]:
                    hit = hit | (rows == row)
                turn = 32 * (place - block) % 128
                merged = jnp.where(hit, pltpu.roll(base, turn, 1) if turn else base, merged)
            total = jnp.where(lanes == place, merged, total)
        return total

    for copy in copies:
        copy.wait()
    fields = [x_ref[c].reshape(cells, length).astype(jnp.bfloat16) for c in range(3)]
    planes = [mxu(wv[...], field) for field in fields]
    wide = [field.astype(jnp.float32) for field in fields]
    count = wp.shape[0]
    weights = jnp.concatenate([wp[...], wp[...]], axis=1)
    for pair, (i, j) in enumerate(INDEX_PAIRS):
        product = wide[i] * wide[j]
        high = product.astype(jnp.bfloat16)
        low = (product - high.astype(jnp.float32)).astype(jnp.bfloat16)
        pair_ref[pl.ds(pair, count, stride=8), :] = mxu(
            weights, jnp.concatenate([high, low], axis=0)
        )

    def along_line(value, line):
        high, middle, low = three_parts(value)
        return mxu(
            jnp.concatenate([high, middle], axis=1), jnp.concatenate([line, line], axis=0)
        ) + mxu(low, line)

    narrow = along_line(
        jnp.concatenate([plane[:32] for plane in planes] + [pair_ref[pl.ds(0, 32), :]], axis=0),
        la[...],
    )
    broad = along_line(
        jnp.concatenate([plane[32:] for plane in planes] + [pair_ref[pl.ds(32, 128), :]], axis=0),
        lb[...],
    )
    for c in range(3):
        value = gathered(narrow[32 * c : 32 * c + 32], ((1, (2,)), (2, (4, 5)), (3, (6,))))
        out_ref[pl.ds(27 + 3 * c, 3), :] = value[0:3]
        out_ref[pl.ds(36 + c, 1), :] = value[3:4]
        out_ref[pl.ds(12 + c, 1), :] = value[4:5]
        out_ref[pl.ds(21 + c, 1), :] = value[5:6]
        out_ref[pl.ds(24 + c, 1), :] = value[6:7]
        for part in range(4):
            at = 128 * c + 32 * part
            base = (0, ROWS + FACE, ROWS + 2 * FACE, ROWS)[part]
            blocks = ((1, (2,)), (2, (4,))) if part else ((1, (2,)),)
            value = gathered(broad[at : at + 32], blocks)
            out_ref[pl.ds(base + 3 * c, 3), :] = value[0:3]
            out_ref[pl.ds(base + 9 + c, 1), :] = value[3:4]
            if part:
                live, still = (12, 21) if part < 3 else (21, 12)
                out_ref[pl.ds(base + live + c, 1), :] = value[4:5]
                out_ref[pl.ds(base + still + c, 1), :] = jnp.zeros((1, 128), jnp.float32)
    out_ref[pl.ds(39, 6), :] = gathered(narrow[96:128], ())[:6]
    out_ref[pl.ds(45, 3), :] = jnp.zeros((3, 128), jnp.float32)
    for part in range(4):
        base = (0, ROWS + FACE, ROWS + 2 * FACE, ROWS)[part]
        out_ref[pl.ds(base + 15, 6), :] = gathered(broad[384 + 32 * part : 416 + 32 * part], ())[:6]


def features_kernel(own_ref, one_ref, swap_ref, both_ref, z_out, gram_ref, b_ref, a_ref, z_ref):
    mine = lax.axis_index("gy")
    chips = b_ref.shape[0]
    in_order(b_ref, mine, (own_ref, one_ref, swap_ref, both_ref), False)
    lane = lax.broadcasted_iota(jnp.int32, (FACE, 128), 1)
    upper = (lane // 32) % 2 == 1
    z_ref[:, 96:, :] = jnp.zeros((chips, 32, 128), jnp.float32)
    for chip in range(chips):
        after = pltpu.roll(b_ref[(chip + 1) % chips, ROWS:, :], 96, 1)
        before = pltpu.roll(b_ref[(chip - 1) % chips, ROWS:, :], 32, 1)
        sums = b_ref[chip, :FACE, :] + jnp.where(upper, after, before)
        base = 27 * chip
        a_ref[pl.ds(base, 9), :] = b_ref[chip, 27:36, :]
        a_ref[pl.ds(base + 9, 3, stride=3), :] = sums[12:15]
        a_ref[pl.ds(base + 10, 3, stride=3), :] = sums[21:24]
        a_ref[pl.ds(base + 11, 3, stride=3), :] = b_ref[chip, 24:27, :]
        a_ref[pl.ds(base + 18, 9), :] = sums[0:9]
        for at, centres, products, width in (
            (90, b_ref[chip, 36:39, :], b_ref[chip, 39:45, :], 3.0),
            (96, sums[9:12], sums[15:21], 12.0),
        ):
            means = [centres[c : c + 1] * (1.0 / width**3) for c in range(3)]
            for pair, (i, j) in enumerate(INDEX_PAIRS):
                z_ref[chip, pl.ds(at + pair, 1), :] = (
                    products[pair : pair + 1] * (1.0 / width**3) - means[i] * means[j]
                )
    total = 3 * chips
    width = lax.broadcasted_iota(jnp.int32, (total, 128), 0) % 3
    factor = jnp.where(width == 0, 1.0 / 12.0, jnp.where(width == 1, 1.0 / 24.0, 1.0 / 48.0))
    grad = [
        [a_ref[pl.ds(3 * i + j, total, stride=9), :] * factor for j in range(3)] for i in range(3)
    ]
    strain = [[None] * 3 for _ in range(3)]
    spin = [[None] * 3 for _ in range(3)]
    for i in range(3):
        for j in range(i, 3):
            strain[i][j] = strain[j][i] = (grad[i][j] + grad[j][i]) * 0.5
            if i != j:
                spin[i][j] = (grad[i][j] - grad[j][i]) * 0.5
                spin[j][i] = (grad[j][i] - grad[i][j]) * 0.5

    def entry(left, right, i, j):
        terms = [
            left[i][k] * right[k][j]
            for k in range(3)
            if left[i][k] is not None and right[k][j] is not None
        ]
        return sum(terms[1:], terms[0])

    squares = [strain[i][j] * strain[i][j] for i in range(3) for j in range(3)]
    magnitude = sum(squares[1:], squares[0])
    columns = [strain[i][j] for i, j in INDEX_PAIRS]
    columns += [entry(strain, strain, i, j) for i, j in INDEX_PAIRS]
    columns += [entry(strain, spin, i, j) - entry(spin, strain, i, j) for i, j in INDEX_PAIRS]
    columns += [entry(spin, spin, i, j) for i, j in INDEX_PAIRS]
    columns += [magnitude * strain[i][j] for i, j in INDEX_PAIRS]
    for index, column in enumerate(columns):
        for chip in range(chips):
            z_ref[chip, pl.ds(index, 3, stride=30), :] = column[3 * chip : 3 * chip + 3]
    z_out[...] = z_ref[mine]
    stacked = jnp.concatenate([z_ref[chip] for chip in range(chips)], axis=1)
    gram = lax.dot_general(
        stacked[:104],
        stacked,
        (((1,), (1,)), ((), ())),
        precision=PRECISE,
        preferred_element_type=jnp.float32,
    )
    rows = lax.broadcasted_iota(jnp.int32, (8, 128), 0)
    lane = lax.broadcasted_iota(jnp.int32, (8, 128), 1)
    gram_ref[pl.ds(0, 8), :] = gram[:8]
    for p in range(1, 7):
        lower = pltpu.roll(gram[48 + 8 * p : 56 + 8 * p], 72, 1)
        gram_ref[pl.ds(8 * p, 8), :] = jnp.where(
            lane >= rows + 8 * p, gram[8 * p : 8 * p + 8], lower
        )


def solve_kernel(total, own_ref, one_ref, swap_ref, both_ref, z_ref, res_ref, coef_ref, g_ref):
    core = lax.axis_index("gz")
    in_order(g_ref, lax.axis_index("gx"), (own_ref, one_ref, swap_ref, both_ref), True)
    packed = [
        (g_ref[0, pl.ds(8 * i, 8), :] + g_ref[1, pl.ds(8 * i, 8), :])
        + (g_ref[2, pl.ds(8 * i, 8), :] + g_ref[3, pl.ds(8 * i, 8), :])
        for i in range(7)
    ]
    one = jnp.where(core >= 0, 1.0, 2.0)
    count, group = 12, 2
    rows = lax.broadcasted_iota(jnp.int32, (8, 128), 0)
    lane = lax.broadcasted_iota(jnp.int32, (8, 128), 1)
    half = []
    for i in range(count + 1):
        if i < 7:
            value = packed[i]
            half.append(jnp.where(lane >= rows + 8 * i, value, 0.0))
        else:
            value = pltpu.roll(packed[i - 6], 56, 1)
            half.append(jnp.where((lane >= 56) & (lane <= rows + 8 * i), value, 0.0))
    blank = [jnp.zeros((8, 128), jnp.float32)]
    other = jnp.transpose(jnp.concatenate(half + blank * (15 - count), axis=0))
    block = []
    for i in range(count + 1):
        value = half[i]
        ridge = value + 0.1 * (value + total * 1e-06) if i < count else value
        value = value + other[8 * i : 8 * i + 8]
        block.append(jnp.where(lane == rows + 8 * i, ridge, value))
    diag = jnp.sum(jnp.where(lane == rows + 96, block[count], 0.0), axis=1, keepdims=True)
    scale = jnp.broadcast_to(jnp.sqrt(diag / total + 1e-06), (8, 128))

    def spread(value, column):
        return jnp.broadcast_to(value[:, column : column + 1], (8, 128))

    def row_of(parts, row):
        return jnp.broadcast_to(parts[row // 8][row % 8 : row % 8 + 1, :], (8, 128))

    for start in range(0, count, group):
        size = 8 * group
        first = 8 * start
        near = range(start + group, min(start + 2 * group, count + 1))
        far = range(start + 2 * group, count + 1)
        square = [[spread(block[start + p], first + m) * one for p in range(group)] for m in range(size)]
        below = {i: [spread(block[i], first + m) for m in range(size)] for i in near}
        inside = (lane >= first) & (lane < first + size)
        panel = []
        for p in range(group):
            unit = (lane == rows + first + 8 * p).astype(jnp.float32)
            panel.append(jnp.where(inside, -unit, block[start + p]))
        inverses = []
        for m in range(size):
            inverses.append(1.0 / row_of(square[m], m))
            factor = [
                jnp.where(rows == m - 8 * p, 0.0, square[m][p]) if m // 8 == p else square[m][p]
                for p in range(group)
            ]
            for k in range(m + 1, size):
                line = row_of(square[k], m) * inverses[m]
                square[k] = [square[k][p] - factor[p] * line for p in range(group)]
            line = row_of(panel, m) * inverses[m]
            panel = [panel[p] - factor[p] * line for p in range(group)]
        lines = [row_of(panel, m) * inverses[m] for m in range(size)]
        for i in near:
            terms = [below[i][m] * lines[m] for m in range(size)]
            while len(terms) > 1:
                terms = [terms[t] + terms[t + 1] for t in range(0, len(terms), 2)]
            block[i] = jnp.where(inside, 0.0, block[i]) - terms[0]
        if far:
            scaled = []
            for p in range(group):
                inverse = inverses[8 * p]
                for row in range(1, 8):
                    inverse = jnp.where(rows == row, inverses[8 * p + row], inverse)
                scaled.append(panel[p] * inverse)
            blank = [jnp.zeros((8, 128), jnp.float32)]
            right = jnp.concatenate(blank * start + scaled + blank * (16 - group - start), axis=0)
            left = jnp.concatenate([jnp.where(inside, block[i], 0.0) for i in far], axis=0)
            change = jnp.dot(left, right, precision=PRECISE, preferred_element_type=jnp.float32)
            for at, i in enumerate(far):
                block[i] = jnp.where(inside, 0.0, block[i]) - change[8 * at : 8 * at + 8]
    answer = jnp.where(lane < 96, block[count], 0.0)
    coef_ref[...] = answer[:6, :96]
    predicted = jnp.dot(answer, z_ref[...], precision=PRECISE, preferred_element_type=jnp.float32)
    residual = (z_ref[pl.ds(96, 8), :] - predicted) / scale
    picked = jnp.zeros((8, 128), jnp.float32)
    for place in range(4):
        even = pltpu.roll(residual, (128 - 16 * place) % 128, 1) if place else residual
        odd = pltpu.roll(residual, 112 - 16 * place, 1)
        picked = jnp.where(lane // 16 == place, jnp.where(core == 0, even, odd), picked)
    res_ref[...] = picked[:6, :64]


def crosswise(value, axis, target):
    pairs = []
    for chip in range(lax.axis_size(axis)):
        for core in range(2):
            pairs.append((2 * chip + core, 2 * target(chip) + 1 - core))
    return lax.ppermute(value, (axis, "gz"), pairs)


def moved(value, axis, step):
    size = lax.axis_size(axis)
    return crosswise(value, axis, lambda chip: (chip + step) % size)


def gathered_over(value, axis, straight):
    pairs = []
    for chip in range(lax.axis_size(axis)):
        if straight:
            pairs += [(2 * chip, 2 * (chip ^ 1)), (2 * chip + 1, 2 * (chip ^ 2) + 1)]
        else:
            pairs += [(2 * chip, 2 * (chip ^ 1) + 1), (2 * chip + 1, 2 * (chip ^ 2))]
    both = crosswise(value, axis, lambda chip: chip ^ 3)
    one = lax.ppermute(value, (axis, "gz"), pairs)
    return value, one, lax.ppermute(one, "gz", [(0, 1), (1, 0)]), both


def in_order(target_ref, mine, refs, straight):
    core = lax.axis_index("gz")
    first = 1 + core if straight else 2 - core
    own_ref, one_ref, swap_ref, both_ref = refs
    target_ref[mine] = own_ref[...]
    target_ref[jnp.bitwise_xor(mine, first)] = one_ref[...]
    target_ref[jnp.bitwise_xor(mine, 3 - first)] = swap_ref[...]
    target_ref[jnp.bitwise_xor(mine, 3)] = both_ref[...]


def call(kernel, outs, scratch, place=pltpu.VMEM):
    def run(*args):
        return pl.pallas_call(
            kernel,
            out_shape=[jax.ShapeDtypeStruct(shape, jnp.float32) for shape in outs],
            in_specs=[pl.BlockSpec(memory_space=place)] * len(args),
            out_specs=[pl.BlockSpec(memory_space=pltpu.VMEM)] * len(outs),
            scratch_shapes=scratch,
            compiler_params=pltpu.CompilerParams(vmem_limit_bytes=8 * 2**20),
        )(*args)

    return run


def chip_shards(velocity):
    bx, by, bz = velocity.shape[1:]
    chips = lax.axis_size("gy")
    length = bz * lax.axis_size("gz")
    low_type, wide_type = jnp.bfloat16, jnp.float32
    tables = [
        velocity_plane_table(bx, by),
        pair_plane_table(bx, by),
        line_table(length, ((3.0, False), (3.0, True), (6.0, False), (6.0, True))),
        line_table(length, ((12.0, False), (12.0, True), (6.0, False), (0.0, False))),
    ]
    tables = [jnp.asarray(table, low_type) for table in tables]
    shapes = [tables[0].shape, tables[1].shape, (bz, 128), (bz, 128)]
    (part,) = call(
        sums_kernel,
        [(ROWS + 3 * FACE, 128)],
        [pltpu.VMEM(velocity.shape, wide_type)]
        + [pltpu.VMEM(shape, low_type) for shape in shapes]
        + [pltpu.VMEM((8 * shapes[1][0], 128), wide_type), pltpu.SemaphoreType.DMA((7,))],
        pltpu.HBM,
    )(*[pltpu.with_memory_space_constraint(value, pltpu.HBM) for value in (velocity, *tables)])
    part = part + lax.ppermute(part, "gz", [(0, 1), (1, 0)])
    own = part[: ROWS + FACE]
    low = moved(part[ROWS + FACE : ROWS + 2 * FACE], "gx", -1)
    high = moved(part[ROWS + 2 * FACE :], "gx", 1)
    left = jnp.arange(128, dtype=jnp.int32)[None, :] < 64
    middle = jnp.zeros((ROWS - FACE, 128), wide_type)
    own = own + jnp.concatenate(
        [jnp.where(left, high, low), middle, jnp.where(left, low, high)], axis=0
    )

    sums = gathered_over(own, "gy", False)
    stacked, gram = call(
        features_kernel,
        [(128, 128), (56, 128)],
        [
            pltpu.VMEM((chips, ROWS + FACE, 128), wide_type),
            pltpu.VMEM((27 * chips, 128), wide_type),
            pltpu.VMEM((chips, 128, 128), wide_type),
        ],
    )(*sums)
    grams = gathered_over(gram, "gx", True)
    samples = (bx // 8) * (by // 8) * (length // 8)
    total = float(samples * lax.axis_size("gx") * chips)
    residual, coefficients = call(
        functools.partial(solve_kernel, total), [(6, 64), (6, 96)], [pltpu.VMEM((4, 56, 128), wide_type)]
    )(*grams, stacked)
    return (residual, coefficients.T)


def chip_form(mesh, velocity):
    shape = mesh.shape
    brick = (velocity.shape[1] // shape["gx"], velocity.shape[2] // shape["gy"])
    return (
        shape["gx"] == shape["gy"] == 4 and shape["gz"] == 2
        and brick == (16, 16) and velocity.shape[3] == 256
    )


def solution(mesh):
    in_specs = (P(None, "gx", "gy", "gz"),)
    out_specs = (P(None, ("gx", "gy", "gz")), P())

    def run(velocity):
        body = chip_shards if chip_form(mesh, velocity) else shards
        return jax.shard_map(
            body, mesh=mesh, in_specs=in_specs, out_specs=out_specs, check_vma=False
        )(velocity)

    return run
```
